128 devices in a mesh: expert: 64 (over y, z, x), half: 2 (over core).
Axes of the slice: x: 4, y: 4, z: 4, core: 2. Of those that a mesh axis runs over, the one named last changes fastest.
Arguments:
- hidden_in: bfloat16 [8192, 2048], P('expert'), may hold values from -6 to 6
- modality: int32 [8192], replicated, may hold values from 0 to 1, as said below
- expert_ids: int32 [8192, 8], P('expert'), may hold values from 0 to 63, all different within a row; in each aligned block of 128 rows (0 to 127, 128 to 255, ...) at most 24 rows name the same one
- route_weights: float32 [8192, 8], P('expert'), may hold values from 0.03 to 0.3
- w_gate_up: bfloat16 [128, 2048, 2, 768], P('expert', None, None, 'half'), may hold values from -0.125 to 0.125
- w_down: bfloat16 [128, 768, 2048], P('expert', 'half'), may hold values from -0.21875 to 0.21875
- norm_gain: float32 [2048], replicated, may hold values from 0.1 to 1.9
- w_query: bfloat16 [2048, 4096], P(None, 'half'), may hold values from -1 to 1
- key_value_weight: bfloat16 [2048, 2, 512], P(None, None, 'half'), may hold values from -1 to 1
- q_gain: float32 [128], replicated, may hold values from 1 to 8
- k_gain: float32 [128], replicated, may hold values from 1 to 8
Outputs:
- hidden_out: float32 [8192, 2048], P('expert')
- attended: bfloat16 [8192, 4096], P('expert', 'half')
The draws below stay inside these ranges and needn't reach their ends.
Inputs may be any that keep to these rules, and one draw needn't show every extreme that they name: `modality`: constant over each aligned block of 128 tokens; both values occur. `expert_ids`: the 8 ids of a token differ; among the tokens of one aligned block of 128 no id is named more than 24 times, a bound that some block reaches.
All inputs are finite; a program needn't handle non-finite values.
Results may differ from the reference program's by a relative error of at most 0.03.
The reference program's roundings to bfloat16 on the way count: a program that leaves them out, or rounds other values in their place, can miss the bound.
Values may be sent and summed in bfloat16 or wider, within the bound.
A program may use at most 128 MiB of HBM per device.

```python
import math
import jax
import jax.numpy as jnp
import numpy as np
from jax import lax

MODEL_DIMENSION = 2048
FF = 768
QUERY_HEADS = 32
KEY_VALUE_HEADS = 4
HEAD_SIZE = 128
TOPK = 8
EXP_DEV = 2
TOK_DEV = 128
EXPERTS = 128
SEQUENCE_TOKENS = 8192
CAP = 24
N_EXPERT = 64
N_HALF = 2


def query_start(key):
    return jax.random.normal(jax.random.fold_in(key, 11), (MODEL_DIMENSION, QUERY_HEADS * HEAD_SIZE), jnp.float32) * MODEL_DIMENSION ** (-0.5)


def draw_w_query(key, part):
    return query_start(key).astype(jnp.bfloat16)


def draw_key_value_weight(key, part):
    key_portion = jax.random.normal(jax.random.fold_in(key, 12), (MODEL_DIMENSION, KEY_VALUE_HEADS * HEAD_SIZE), jnp.float32) * MODEL_DIMENSION ** (-0.5)
    value_portion = jax.random.normal(jax.random.fold_in(key, 13), (MODEL_DIMENSION, KEY_VALUE_HEADS * HEAD_SIZE), jnp.float32) * MODEL_DIMENSION ** (-0.5)
    return jnp.stack([key_portion, value_portion], axis=1).astype(jnp.bfloat16)


def gain_draw(key, salt):
    return jnp.exp(jax.random.uniform(jax.random.fold_in(key, salt), (HEAD_SIZE,), jnp.float32, 0.0, math.log(4.0)))


def draw_q_gain(key, part):
    return gain_draw(key, 21)


def draw_k_gain(key, part):
    return gain_draw(key, 22)


def draw_modality(key, part):
    block_count = SEQUENCE_TOKENS // TOK_DEV
    picks = jax.random.randint(jax.random.fold_in(key, 31), (block_count,), 0, 10)
    kinds = (picks < 7).astype(jnp.int32)
    kinds = kinds.at[0].set(0).at[1].set(1)
    return jnp.repeat(kinds, TOK_DEV, total_repeat_length=SEQUENCE_TOKENS)


def steps_of(own_key, dims, split, least, largest):
    def one(position, shards_of):
        steps = jax.random.uniform(jax.random.fold_in(jax.random.fold_in(own_key, 6), position), (shards_of,), jnp.float32, least / len(split), largest / len(split))
        return jnp.repeat(jnp.exp(steps), dims[position] // shards_of).reshape((-1,) + (1,) * (len(dims) - position - 1))

    level = one(*split[0])
    for cut in split[1:]:
        level = level * one(*cut)
    return level


def deal_out(own_key, own, number, rows, count, top, most, lean):
    order = jax.random.permutation(own_key, count)
    packed, common = portions_of(count, rows * top, most, lean, True), portions_of(count, rows * top, most, lean, False)
    places = jnp.arange(count)

    def named(sizes, rotation):
        used = int((sizes > 0).sum())
        fixed = max(1, used // 4)
        passed = fixed + (places - fixed + rotation * (used - fixed)) % max(1, count - fixed)
        return jnp.zeros((count,), jnp.int32).at[order[jnp.where(places < fixed, places, passed)]].set(jnp.asarray(sizes, jnp.int32))

    sizes = jnp.where(number % 4 == 0, named(packed, number // 4), named(common, number - number // 4 - 1))
    mixed = jax.random.permutation(jax.random.fold_in(own, 3), count)
    giver, taker = mixed[0:count // 2 * 2:2], mixed[1:count // 2 * 2:2]
    room = jnp.minimum(sizes[giver] - 1, most - sizes[taker]) // 2
    room = jnp.where((giver == order[0]) | (taker == order[0]) | (sizes[taker] == 0), 0, jnp.maximum(room, 0))
    passed = jax.random.randint(jax.random.fold_in(own, 4), (count // 2,), 0, 1 << 20) % (room + 1)
    sizes = sizes.at[giver].add(-passed).at[taker].add(passed)
    items = jnp.searchsorted(jnp.cumsum(sizes), jnp.arange(rows * top), side="right").astype(jnp.int32)
    grid = items.reshape(top, rows).T
    grid = grid[jax.random.permutation(jax.random.fold_in(own, 1), rows)]
    rotation = jax.random.randint(jax.random.fold_in(own, 2), (rows, 1), 0, top)
    return jnp.take_along_axis(grid, (jnp.arange(top)[None, :] + rotation) % top, axis=1)


def portions_of(count, total, reach, slope, full):
    weights = [(1 << 20) // math.isqrt(standing ** slope) + 1 for standing in range(1, count + 1)]
    largest = reach if full else min(reach, max(-(-total // count), total * weights[0] // sum(weights)))
    least = 1 if total - largest >= count - 1 else 0
    holding, surplus = [largest] + [least] * (count - 1), total - largest - least * (count - 1)
    while surplus > 0:
        free = [i for i in range(1, count) if holding[i] < largest] or [i for i in range(1, count) if holding[i] < reach]
        mass, remaining = sum([weights[i] for i in free]), surplus
        for i in free:
            more = min(reach - holding[i], max(1, remaining * weights[i] // mass), surplus)
            holding[i] = holding[i] + more
            surplus = surplus - more
    return np.array(holding)


def scatter_about(stream_key, shape, deviation, limit, split=(), kind=jnp.bfloat16):
    loudness = steps_of(stream_key, shape, split, -0.22, 0.18) if split else 1.0
    values = jax.random.normal(stream_key, shape, jnp.float32) * deviation * loudness
    return jnp.minimum(jnp.maximum(values, -limit), limit).astype(kind)


def setup_inputs(seed: int = 0) -> dict:
    splits = jax.random.split(jax.random.key(seed), 12)
    hidden_in = scatter_about(splits[0], (SEQUENCE_TOKENS, MODEL_DIMENSION), 1.0, 6.0, ((0, 64),))
    modality = draw_modality(jax.random.fold_in(splits[11], 71), 0)
    expert_ids_keys = jax.random.split(jax.random.fold_in(splits[2], 1), SEQUENCE_TOKENS // TOK_DEV)
    expert_ids_turns = jax.random.permutation(jax.random.fold_in(splits[2], 3), SEQUENCE_TOKENS // TOK_DEV)
    expert_ids = jax.vmap(lambda own, number: deal_out(jax.random.fold_in(splits[2], 2), own, number, TOK_DEV, N_EXPERT, TOPK, CAP, 2))(expert_ids_keys, expert_ids_turns).reshape((SEQUENCE_TOKENS, TOPK))
    route_weights = jnp.clip(jnp.exp(math.log(0.3) - 2.3025852 * jax.random.uniform(splits[3], (SEQUENCE_TOKENS, TOPK), jnp.float32) ** steps_of(splits[3], (SEQUENCE_TOKENS, TOPK), ((0, 64),), -0.2, 0.2)), 0.03, 0.3)
    w_gate_up = scatter_about(splits[4], (EXPERTS, MODEL_DIMENSION, 2, FF), MODEL_DIMENSION ** -0.5, 0.125, ((0, 64), (3, 2)))
    w_down = scatter_about(splits[5], (EXPERTS, FF, MODEL_DIMENSION), FF ** -0.5, 0.21875, ((0, 64), (1, 2)))
    norm_gain = jnp.clip(1.0 + 0.18 * jax.random.normal(splits[6], (MODEL_DIMENSION,), jnp.float32), 0.1, 1.9)
    w_query = draw_w_query(jax.random.fold_in(splits[11], 71), 0)
    key_value_weight = draw_key_value_weight(jax.random.fold_in(splits[11], 71), 0)
    q_gain = draw_q_gain(jax.random.fold_in(splits[11], 71), 0)
    k_gain = draw_k_gain(jax.random.fold_in(splits[11], 71), 0)
    return dict(hidden_in=hidden_in, modality=modality, expert_ids=expert_ids, route_weights=route_weights, w_gate_up=w_gate_up, w_down=w_down, norm_gain=norm_gain, w_query=w_query, key_value_weight=key_value_weight, q_gain=q_gain, k_gain=k_gain)


EPSILON = 1e-06
tile_rows = 128

def rms_scale(values, gain_row):
    mean_sq = lax.optimization_barrier(jnp.mean(values * values, axis=-1, keepdims=True))
    return values * lax.rsqrt(mean_sq + EPSILON) * gain_row

def moe_block(hidden_in, modality, expert_ids, route_weights, w_gate_up, w_down):
    row_count = SEQUENCE_TOKENS * TOPK
    flat_expert = (EXP_DEV * expert_ids + modality[:, None]).reshape(-1).astype(jnp.int32)
    ordering = jnp.argsort(flat_expert, stable=True).astype(jnp.int32)
    sorted_expert = flat_expert[ordering]
    counts = jnp.zeros((EXPERTS,), jnp.int32).at[flat_expert].add(1)
    starts = (jnp.cumsum(counts) - counts).astype(jnp.int32)
    padded = ((counts + tile_rows - 1) // tile_rows * tile_rows).astype(jnp.int32)
    padded_end = jnp.cumsum(padded).astype(jnp.int32)
    padded_start = (padded_end - padded).astype(jnp.int32)
    positions = (padded_start[sorted_expert] + jnp.arange(row_count, dtype=jnp.int32) - starts[sorted_expert]).astype(jnp.int32)
    tile_count = row_count // tile_rows + 1 + EXPERTS
    source_token = jnp.full((tile_count * tile_rows,), SEQUENCE_TOKENS, jnp.int32).at[positions].set((ordering // TOPK).astype(jnp.int32))
    tile_first = (jnp.arange(tile_count, dtype=jnp.int32) * tile_rows)[:, None]
    tile_expert = jnp.minimum(lax.optimization_barrier(jnp.sum((padded_end[None, :] <= tile_first).astype(jnp.int32), axis=1)), EXPERTS - 1).astype(jnp.int32)
    padded_in = jnp.concatenate([hidden_in, jnp.zeros((1, MODEL_DIMENSION), hidden_in.dtype)], axis=0)
    half_units = FF // N_HALF

    def one_tile(tile_args):
        tile_tokens, expert = tile_args
        rows_in = padded_in[tile_tokens]
        weights_gu = w_gate_up[expert]
        gate_part = jnp.dot(rows_in, weights_gu[:, 0, :], preferred_element_type=jnp.float32)
        upward = jnp.dot(rows_in, weights_gu[:, 1, :], preferred_element_type=jnp.float32)
        activated = (jax.nn.silu(gate_part) * upward).astype(jnp.bfloat16)
        down_rows = w_down[expert]
        summed = jnp.zeros((tile_rows, MODEL_DIMENSION), jnp.float32)
        for half_index in range(N_HALF):
            lower = half_index * half_units
            summed = summed + jnp.dot(activated[:, lower:lower + half_units], down_rows[lower:lower + half_units], preferred_element_type=jnp.float32)
        return summed.astype(jnp.bfloat16)
    tile_out = lax.map(one_tile, (source_token.reshape(tile_count, tile_rows), tile_expert)).reshape(tile_count * tile_rows, MODEL_DIMENSION)
    row_position = jnp.zeros((row_count,), jnp.int32).at[ordering].set(positions)
    routed = tile_out[row_position].astype(jnp.float32).reshape(SEQUENCE_TOKENS, TOPK, MODEL_DIMENSION)
    mixture = lax.optimization_barrier(jnp.sum(routed * route_weights[:, :, None], axis=1))
    return hidden_in.astype(jnp.float32) + mixture

def attention(hidden_out, norm_gain, w_query, key_value_weight, q_gain, k_gain):
    normalized_input = rms_scale(hidden_out, norm_gain).astype(jnp.bfloat16)
    queries = jnp.dot(normalized_input, w_query, preferred_element_type=jnp.float32).reshape(SEQUENCE_TOKENS, QUERY_HEADS, HEAD_SIZE)
    queries = rms_scale(queries, q_gain).astype(jnp.bfloat16)
    key_value_rows = jnp.dot(normalized_input, key_value_weight.reshape(MODEL_DIMENSION, 2 * KEY_VALUE_HEADS * HEAD_SIZE), preferred_element_type=jnp.float32).reshape(SEQUENCE_TOKENS, 2, KEY_VALUE_HEADS, HEAD_SIZE)
    keys_wide = rms_scale(key_value_rows[:, 0], k_gain).astype(jnp.bfloat16).astype(jnp.float32)
    values_wide = key_value_rows[:, 1].astype(jnp.bfloat16).astype(jnp.float32)
    queries_per_group = QUERY_HEADS // KEY_VALUE_HEADS
    rows_per_block = math.gcd(SEQUENCE_TOKENS, 256)
    score_scale = HEAD_SIZE ** (-0.5)

    def one_block(query_tile_rows):
        grouped_queries = query_tile_rows.astype(jnp.float32).reshape(rows_per_block, KEY_VALUE_HEADS, queries_per_group, HEAD_SIZE)
        scores = jnp.einsum('qhgd,khd->hgqk', grouped_queries, keys_wide) * score_scale
        row_peak = lax.optimization_barrier(jnp.max(scores, axis=-1, keepdims=True))
        weights = jnp.exp(scores - row_peak)
        totals = lax.optimization_barrier(jnp.sum(weights, axis=-1, keepdims=True))
        rounded_probs = lax.optimization_barrier(weights.astype(jnp.bfloat16)).astype(jnp.float32)
        mixed_rows = jnp.einsum('hgqk,khd->hgqd', rounded_probs, values_wide) / totals
        return mixed_rows.transpose(2, 0, 1, 3).reshape(rows_per_block, QUERY_HEADS * HEAD_SIZE).astype(jnp.bfloat16)
    attended = lax.map(one_block, queries.reshape(SEQUENCE_TOKENS // rows_per_block, rows_per_block, QUERY_HEADS, HEAD_SIZE))
    return attended.reshape(SEQUENCE_TOKENS, QUERY_HEADS * HEAD_SIZE)

def reference(hidden_in, modality, expert_ids, route_weights, w_gate_up, w_down, norm_gain, w_query, key_value_weight, q_gain, k_gain):
    hidden_out = moe_block(hidden_in, modality, expert_ids, route_weights, w_gate_up, w_down)
    attended = attention(hidden_out, norm_gain, w_query, key_value_weight, q_gain, k_gain)
    return (hidden_out, attended)
```

```python
import functools
import jax
import jax.numpy as jnp
from jax import lax
from jax.experimental import pallas as pl
from jax.experimental.pallas import tpu as pltpu
from jax.sharding import PartitionSpec as P

EPSILON = 1e-06
MESH = pl.DeviceIdType.MESH
F32 = jnp.float32
BF16 = jnp.bfloat16

CHIPS = 64
CAP = 24
TOK = 128
D = 2048
HD = 1024
UNITS = 384
PER = 8
BATCHES = CHIPS // PER
ROWS = PER * CAP


def offsets(n):
    a, b, c = n // 16, (n // 4) % 4, n % 4
    return c, (c + b) % 4, (c + a) % 4


def chip_plus(chip, n):
    oy, oz, ox = offsets(n)
    y, z, x = chip // 16, (chip // 4) % 4, chip % 4
    return ((y + oy) % 4) * 16 + ((z + oz) % 4) * 4 + (x + ox) % 4


def chip_minus(chip, n):
    oy, oz, ox = offsets(n)
    y, z, x = chip // 16, (chip // 4) % 4, chip % 4
    return ((y + 4 - oy) % 4) * 16 + ((z + 4 - oz) % 4) * 4 + (x + 4 - ox) % 4


def slot_group(c):
    return (c * 2731) >> 16


def moe_kernel(
    x_ref, mod_ref, ids_ref, rw_ref, wgu_hbm, wd_hbm, gain_ref, wq_hbm, wkv_hbm, qg_ref, kg_ref,
    ho_ref, q_ref, kv_ref,
    wraw, w_s, wd_s, wq_s, kvraw, kvw_s, out_s, a_s, b_s, ret_s, rin_s, gu_s, own_s, ps_s, pr_s,
    mask_s, val_s, hi_s, lo_s, valt_s, acc_s, nrm_s,
    wsem, dsend, drecv, fsend, frecv, psend, precv, rsend, rrecv, hsend, hrecv,
):
    me = lax.axis_index("expert")
    core = lax.axis_index("half")
    mate = 1 - core
    own = pl.multiple_of(core * HD, HD)
    oth = pl.multiple_of(mate * HD, HD)

    loads = [
        pltpu.make_async_copy(wgu_hbm, wraw, wsem.at[0]),
        pltpu.make_async_copy(wd_hbm, wd_s, wsem.at[1]),
        pltpu.make_async_copy(wkv_hbm, kvraw, wsem.at[2]),
        pltpu.make_async_copy(wq_hbm, wq_s, wsem.at[3]),
    ]
    for load in loads:
        load.start()

    barrier = pltpu.get_barrier_semaphore()
    pl.semaphore_signal(barrier, inc=1, device_id={"expert": me, "half": mate}, device_id_type=MESH)

    @pl.loop(1, CHIPS)
    def _(n):
        pl.semaphore_signal(
            barrier, inc=1, device_id={"expert": chip_plus(me, n), "half": core}, device_id_type=MESH
        )

    lane = lax.broadcasted_iota(jnp.int32, (TOK, TOK), 1)
    row = lax.broadcasted_iota(jnp.int32, (TOK, TOK), 0)
    la, lb, lc = lane >> 4, (lane >> 2) & 3, lane & 3
    my_y, my_z, my_x = me // 16, (me // 4) % 4, me % 4
    dst_row = (
        ((my_y + lc) & 3) * 16 + ((my_z + lc + lb) & 3) * 4 + ((my_x + lc + la) & 3)
    )
    dst_row = jnp.where(lane < CHIPS, dst_row, -1)
    ids = ids_ref[...]
    rw = rw_ref[...]
    member = jnp.zeros((TOK, TOK), F32)
    weight = jnp.zeros((TOK, TOK), F32)
    for j in range(ids.shape[1]):
        hit = jnp.broadcast_to(ids[:, j : j + 1], (TOK, TOK)) == dst_row
        member = member + jnp.where(hit, 1.0, 0.0)
        weight = weight + jnp.where(hit, jnp.broadcast_to(rw[:, j : j + 1], (TOK, TOK)), 0.0)
    lower = jnp.where(lane < row, 1.0, 0.0).astype(BF16)
    rank = jnp.dot(lower, member.astype(BF16), preferred_element_type=F32)
    val = jnp.where(member > 0.5, rank, -1.0)
    val_s[...] = val.astype(BF16)
    valt_s[...] = val.T.astype(BF16)
    high = weight.astype(BF16)
    hi_s[...] = high
    lo_s[...] = (weight - high.astype(F32)).astype(BF16)

    pl.semaphore_wait(barrier, CHIPS)

    x_own = x_ref[:, pl.ds(own, HD)]

    @pl.loop(0, BATCHES)
    def _(b):
        c = lax.broadcasted_iota(jnp.int32, (ROWS, TOK), 0) + b * ROWS
        group = slot_group(c)
        spread = jnp.where(group == lax.broadcasted_iota(jnp.int32, (ROWS, TOK), 1), 1.0, 0.0)
        vals = jnp.dot(spread.astype(BF16), valt_s[...], preferred_element_type=F32)
        pick = jnp.where(vals == (c - CAP * group).astype(F32), 1.0, 0.0).astype(BF16)
        rows_out = jnp.dot(pick, x_own, preferred_element_type=F32).astype(BF16)
        out_s[pl.ds(b * PER, PER)] = rows_out.reshape(PER, CAP, HD)

        @pl.loop(0, PER)
        def _(i):
            n = b * PER + i

            @pl.when(n == 0)
            def _():
                pltpu.make_async_copy(out_s.at[0], a_s.at[0], drecv.at[0]).start()

            @pl.when(n > 0)
            def _():
                pltpu.make_async_remote_copy(
                    src_ref=out_s.at[n],
                    dst_ref=a_s.at[n],
                    send_sem=dsend,
                    recv_sem=drecv.at[b],
                    device_id={"expert": chip_plus(me, n), "half": core},
                    device_id_type=MESH,
                ).start()

    @pl.loop(0, CHIPS)
    def _(n):
        mask_s[n] = jnp.full((CAP, 128), mod_ref[chip_minus(me, n), 0], jnp.int32).astype(F32)

    prow = lax.broadcasted_iota(jnp.int32, (256, 256), 0)
    pcol = lax.broadcasted_iota(jnp.int32, (256, 256), 1)
    part = jnp.where(pcol == jnp.where(prow < 128, 2 * prow, 2 * prow - 255), 1.0, 0.0).astype(BF16)
    loads[0].wait()

    @pl.loop(0, D // 128)
    def _(r):
        r0 = pl.multiple_of(r * 128, 128)
        for e in range(2):
            block = wraw[e, pl.ds(r0, 128)].reshape(256, UNITS)
            parted = jnp.dot(part, block, preferred_element_type=F32).astype(BF16)
            w_s[pl.ds(r0, 128), e * 2 * UNITS : e * 2 * UNITS + UNITS] = parted[:128]
            w_s[pl.ds(r0, 128), e * 2 * UNITS + UNITS : (e + 1) * 2 * UNITS] = parted[128:]

    loads[2].wait()

    @pl.loop(0, D // 128)
    def _(r):
        r0 = pl.multiple_of(r * 128, 128)
        block = kvraw[pl.ds(r0, 128)].reshape(256, 256)
        parted = jnp.dot(part, block, preferred_element_type=F32).astype(BF16)
        kvw_s[pl.ds(r0, 128), 0:256] = parted[:128]
        kvw_s[pl.ds(r0, 128), 256:512] = parted[128:]

    loads[1].wait()

    def pieces(ref, b):
        return ref.at[pl.ds(b * PER, PER)]

    def forward(b):
        pltpu.make_async_copy(pieces(a_s, b), pieces(a_s, b), drecv.at[b]).wait()
        pltpu.make_async_remote_copy(
            src_ref=pieces(a_s, b),
            dst_ref=pieces(b_s, b),
            send_sem=fsend.at[b],
            recv_sem=frecv.at[b],
            device_id={"expert": me, "half": mate},
            device_id_type=MESH,
        ).start()

    forward(0)

    @pl.loop(0, BATCHES)
    def _(b):
        pltpu.make_async_remote_copy(
            src_ref=pieces(a_s, b),
            dst_ref=pieces(b_s, b),
            send_sem=fsend.at[b],
            recv_sem=frecv.at[b],
            device_id={"expert": me, "half": mate},
            device_id_type=MESH,
        ).wait()
        xa = a_s[pl.ds(b * PER, PER)].reshape(ROWS, HD)
        xb = b_s[pl.ds(b * PER, PER)].reshape(ROWS, HD)

        @pl.loop(0, 4)
        def _(k):
            cols = pl.ds(pl.multiple_of(k * UNITS, 128), UNITS)
            gu_s[:, cols] = jnp.dot(
                xa, w_s[pl.ds(own, HD), cols], preferred_element_type=F32
            ) + jnp.dot(xb, w_s[pl.ds(oth, HD), cols], preferred_element_type=F32)

        mask = mask_s[pl.ds(b * PER, PER)].reshape(ROWS, 128)
        image = jnp.concatenate([mask, mask, mask], axis=1) > 0.5
        gate = jnp.where(image, gu_s[:, 2 * UNITS : 3 * UNITS], gu_s[:, :UNITS])
        up = jnp.where(image, gu_s[:, 3 * UNITS :], gu_s[:, UNITS : 2 * UNITS])
        act = gate / (1.0 + jnp.exp(-gate)) * up
        both = jnp.concatenate(
            [jnp.where(image, 0.0, act), jnp.where(image, act, 0.0)], axis=1
        ).astype(BF16)

        ps_s[...] = jnp.dot(both, wd_s[:, pl.ds(oth, HD)], preferred_element_type=F32)
        swap = pltpu.make_async_remote_copy(
            src_ref=ps_s,
            dst_ref=pr_s.at[b % 2],
            send_sem=psend,
            recv_sem=precv.at[b % 2],
            device_id={"expert": me, "half": mate},
            device_id_type=MESH,
        )
        swap.start()
        own_s[...] = jnp.dot(both, wd_s[:, pl.ds(own, HD)], preferred_element_type=F32)
        swap.wait()
        ret_s[pl.ds(b * PER, PER)] = (own_s[...] + pr_s[b % 2]).astype(BF16).reshape(PER, CAP, HD)

        @pl.loop(0, PER)
        def _(i):
            n = b * PER + i

            @pl.when(n == 0)
            def _():
                pltpu.make_async_copy(ret_s.at[0], rin_s.at[0], rrecv.at[0]).start()

            @pl.when(n > 0)
            def _():
                pltpu.make_async_remote_copy(
                    src_ref=ret_s.at[n],
                    dst_ref=rin_s.at[n],
                    send_sem=rsend,
                    recv_sem=rrecv.at[b],
                    device_id={"expert": chip_minus(me, n), "half": core},
                    device_id_type=MESH,
                ).start()

        @pl.when(b < BATCHES - 1)
        def _():
            forward(b + 1)

    acc_s[...] = x_ref[:, pl.ds(own, HD)].astype(F32)
    wide = 2 * ROWS

    @pl.loop(0, BATCHES // 2)
    def _(b):
        c = lax.broadcasted_iota(jnp.int32, (TOK, wide), 1) + b * wide
        group = slot_group(c)
        spread = jnp.where(group == lax.broadcasted_iota(jnp.int32, (TOK, wide), 0), 1.0, 0.0).astype(BF16)
        vals = jnp.dot(val_s[...], spread, preferred_element_type=F32)
        pick = vals == (c - CAP * group).astype(F32)
        w_hi = jnp.where(pick, jnp.dot(hi_s[...], spread, preferred_element_type=F32), 0.0).astype(BF16)
        w_lo = jnp.where(pick, jnp.dot(lo_s[...], spread, preferred_element_type=F32), 0.0).astype(BF16)
        for k in range(2):
            pltpu.make_async_copy(pieces(rin_s, 2 * b + k), pieces(rin_s, 2 * b + k), rrecv.at[2 * b + k]).wait()
        back = rin_s[pl.ds(b * 2 * PER, 2 * PER)].reshape(wide, HD)
        acc_s[...] += jnp.dot(w_hi, back, preferred_element_type=F32) + jnp.dot(
            w_lo, back, preferred_element_type=F32
        )

    ho_ref[:, pl.ds(own, HD)] = acc_s[...]
    share = pltpu.make_async_remote_copy(
        src_ref=acc_s,
        dst_ref=ho_ref.at[:, pl.ds(own, HD)],
        send_sem=hsend,
        recv_sem=hrecv,
        device_id={"expert": me, "half": mate},
        device_id_type=MESH,
    )
    share.start()
    loads[3].wait()
    share.wait()
    hidden = ho_ref[...]
    mean_sq = jnp.mean(hidden * hidden, axis=-1, keepdims=True)
    nrm_s[...] = (hidden * lax.rsqrt(mean_sq + EPSILON) * gain_ref[...]).astype(BF16)

    def head_norm(values, gain):
        scale = lax.rsqrt(jnp.mean(values * values, axis=-1, keepdims=True) + EPSILON)
        return (values * scale * gain).astype(BF16)

    @pl.loop(0, 4)
    def _(k):
        kv = jnp.dot(nrm_s[...], kvw_s[:, pl.ds(pl.multiple_of(k * 128, 128), 128)], preferred_element_type=F32)

        @pl.when(k < 2)
        def _():
            kv_ref[k] = head_norm(kv, kg_ref[...])

        @pl.when(k >= 2)
        def _():
            kv_ref[k] = kv.astype(BF16)

    @pl.loop(0, 8)
    def _(k):
        q2 = jnp.dot(nrm_s[...], wq_s[:, pl.ds(pl.multiple_of(k * 256, 256), 256)], preferred_element_type=F32)
        q_ref[2 * k] = head_norm(q2[:, :128], qg_ref[...])
        q_ref[2 * k + 1] = head_norm(q2[:, 128:], qg_ref[...])

    rest = pl.ds(1, CHIPS - 1)
    pltpu.make_async_copy(out_s.at[rest], out_s.at[rest], dsend).wait()
    pltpu.make_async_copy(ret_s.at[rest], ret_s.at[rest], rsend).wait()


def moe_call(x, mod, ids, rw, wgu, wd, gain, wq, wkv, qg, kg):
    vm = pl.BlockSpec(memory_space=pltpu.VMEM)
    hbm = pl.BlockSpec(memory_space=pl.ANY)
    sm = pl.BlockSpec(memory_space=pltpu.SMEM)
    dma = pltpu.SemaphoreType.DMA
    return pl.pallas_call(
        moe_kernel,
        out_shape=(
            jax.ShapeDtypeStruct((TOK, D), F32),
            jax.ShapeDtypeStruct((16, TOK, 128), BF16),
            jax.ShapeDtypeStruct((4, TOK, 128), BF16),
        ),
        in_specs=[vm, sm, vm, vm, hbm, hbm, vm, hbm, hbm, vm, vm],
        out_specs=(vm, vm, vm),
        scratch_shapes=[
            pltpu.VMEM((2, D, 2, UNITS), BF16),
            pltpu.VMEM((D, 4 * UNITS), BF16),
            pltpu.VMEM((2 * UNITS, D), BF16),
            pltpu.VMEM((D, D), BF16),
            pltpu.VMEM((D, 2, 256), BF16),
            pltpu.VMEM((D, 512), BF16),
            pltpu.VMEM((CHIPS, CAP, HD), BF16),
            pltpu.VMEM((CHIPS, CAP, HD), BF16),
            pltpu.VMEM((CHIPS, CAP, HD), BF16),
            pltpu.VMEM((CHIPS, CAP, HD), BF16),
            pltpu.VMEM((CHIPS, CAP, HD), BF16),
            pltpu.VMEM((ROWS, 4 * UNITS), F32),
            pltpu.VMEM((ROWS, HD), F32),
            pltpu.VMEM((ROWS, HD), F32),
            pltpu.VMEM((2, ROWS, HD), F32),
            pltpu.VMEM((CHIPS, CAP, 128), F32),
            pltpu.VMEM((TOK, TOK), BF16),
            pltpu.VMEM((TOK, TOK), BF16),
            pltpu.VMEM((TOK, TOK), BF16),
            pltpu.VMEM((TOK, TOK), BF16),
            pltpu.VMEM((TOK, HD), F32),
            pltpu.VMEM((TOK, D), BF16),
            dma((4,)),
            dma,
            dma((BATCHES,)),
            dma((BATCHES,)),
            dma((BATCHES,)),
            dma,
            dma((2,)),
            dma,
            dma((BATCHES,)),
            dma,
            dma,
        ],
        compiler_params=pltpu.CompilerParams(
            collective_id=0, has_side_effects=True, vmem_limit_bytes=62 * 1024 * 1024
        ),
    )(x, mod, ids, rw, wgu, wd, gain, wq, wkv, qg, kg)


def body(hidden_in, modality, expert_ids, route_weights, w_gate_up, w_down, norm_gain, w_query,
         key_value_weight, q_gain, k_gain):
    hidden_out, queries, kv_block = moe_call(
        hidden_in, modality.reshape(CHIPS, TOK), expert_ids, route_weights, w_gate_up,
        w_down.reshape(2 * UNITS, D), norm_gain.reshape(1, D), w_query, key_value_weight,
        q_gain.reshape(1, 128), k_gain.reshape(1, 128),
    )
    grouped = queries.reshape(2, 8 * TOK, 128)
    gathered = lax.all_gather(kv_block, "expert", axis=1, tiled=True)
    scores = jnp.einsum("hrd,hkd->hrk", grouped, gathered[:2], preferred_element_type=F32) * 128**-0.5
    peak = jnp.max(scores, axis=-1, keepdims=True)
    weights = jnp.exp(scores - peak)
    totals = jnp.sum(weights, axis=-1, keepdims=True)
    mixed = jnp.einsum("hrk,hkd->hrd", weights.astype(BF16), gathered[2:], preferred_element_type=F32) / totals
    attended = mixed.reshape(16, TOK, 128).transpose(1, 0, 2).reshape(TOK, D).astype(BF16)
    return hidden_out, attended


def solution(mesh):
    in_specs = (
        P("expert", None), P(), P("expert", None), P("expert", None),
        P("expert", None, None, "half"), P("expert", "half", None), P(), P(None, "half"),
        P(None, None, "half"), P(), P(),
    )
    out_specs = (P("expert", None), P("expert", "half"))
    return jax.shard_map(body, mesh=mesh, in_specs=in_specs, out_specs=out_specs, check_vma=False)
```

```python
import functools
import jax
import jax.numpy as jnp
from jax import lax
from jax.experimental import pallas as pl
from jax.experimental.pallas import tpu as pltpu
from jax.sharding import PartitionSpec as P

EPSILON = 1e-06
MESH = pl.DeviceIdType.MESH
F32 = jnp.float32
BF16 = jnp.bfloat16

CHIPS = 64
CAP = 24
TOK = 128
D = 2048
HD = 1024
UNITS = 384
PER = 8
BATCHES = CHIPS // PER
ROWS = PER * CAP


def offsets(n):
    a, b, c = n // 16, (n // 4) % 4, n % 4
    return c, (c + b) % 4, (c + a) % 4


def chip_plus(chip, n):
    oy, oz, ox = offsets(n)
    y, z, x = chip // 16, (chip // 4) % 4, chip % 4
    return ((y + oy) % 4) * 16 + ((z + oz) % 4) * 4 + (x + ox) % 4


def chip_minus(chip, n):
    oy, oz, ox = offsets(n)
    y, z, x = chip // 16, (chip // 4) % 4, chip % 4
    return ((y + 4 - oy) % 4) * 16 + ((z + 4 - oz) % 4) * 4 + (x + 4 - ox) % 4


def slot_group(c):
    return (c * 2731) >> 16


def moe_kernel(
    x_ref, mod_ref, ids_ref, rw_ref, wgu_hbm, wd_hbm, gain_ref, wq_hbm, wkv_hbm, qg_ref, kg_ref,
    ho_ref, q_ref, kv_ref,
    wraw, w_s, wd_s, wq_s, kvraw, kvw_s, out_s, a_s, b_s, ret_s, rin_s, gu_s, own_s, ps_s, pr_s,
    mask_s, val_s, hi_s, lo_s, valt_s, acc_s, nrm_s,
    wsem, dsend, drecv, fsend, frecv, psend, precv, rsend, rrecv, hsend, hrecv,
):
    me = lax.axis_index("expert")
    core = lax.axis_index("half")
    mate = 1 - core
    own = pl.multiple_of(core * HD, HD)
    oth = pl.multiple_of(mate * HD, HD)

    loads = [
        pltpu.make_async_copy(wgu_hbm, wraw, wsem.at[0]),
        pltpu.make_async_copy(wd_hbm, wd_s, wsem.at[1]),
        pltpu.make_async_copy(wkv_hbm, kvraw, wsem.at[2]),
        pltpu.make_async_copy(wq_hbm, wq_s, wsem.at[3]),
    ]
    for load in loads:
        load.start()

    barrier = pltpu.get_barrier_semaphore()
    pl.semaphore_signal(barrier, inc=1, device_id={"expert": me, "half": mate}, device_id_type=MESH)

    @pl.loop(1, CHIPS)
    def _(n):
        pl.semaphore_signal(
            barrier, inc=1, device_id={"expert": chip_plus(me, n), "half": core}, device_id_type=MESH
        )

    lane = lax.broadcasted_iota(jnp.int32, (TOK, TOK), 1)
    row = lax.broadcasted_iota(jnp.int32, (TOK, TOK), 0)
    la, lb, lc = lane >> 4, (lane >> 2) & 3, lane & 3
    my_y, my_z, my_x = me // 16, (me // 4) % 4, me % 4
    dst_row = (
        ((my_y + lc) & 3) * 16 + ((my_z + lc + lb) & 3) * 4 + ((my_x + lc + la) & 3)
    )
    dst_row = jnp.where(lane < CHIPS, dst_row, -1)
    ids = ids_ref[...]
    rw = rw_ref[...]
    member = jnp.zeros((TOK, TOK), F32)
    weight = jnp.zeros((TOK, TOK), F32)
    for j in range(ids.shape[1]):
        hit = jnp.broadcast_to(ids[:, j : j + 1], (TOK, TOK)) == dst_row
        member = member + jnp.where(hit, 1.0, 0.0)
        weight = weight + jnp.where(hit, jnp.broadcast_to(rw[:, j : j + 1], (TOK, TOK)), 0.0)
    lower = jnp.where(lane < row, 1.0, 0.0).astype(BF16)
    rank = jnp.dot(lower, member.astype(BF16), preferred_element_type=F32)
    val = jnp.where(member > 0.5, rank, -1.0)
    val_s[...] = val.astype(BF16)
    valt_s[...] = val.T.astype(BF16)
    high = weight.astype(BF16)
    hi_s[...] = high
    lo_s[...] = (weight - high.astype(F32)).astype(BF16)

    pl.semaphore_wait(barrier, CHIPS)

    x_own = x_ref[:, pl.ds(own, HD)]

    @pl.loop(0, BATCHES)
    def _(b):
        c = lax.broadcasted_iota(jnp.int32, (ROWS, TOK), 0) + b * ROWS
        group = slot_group(c)
        spread = jnp.where(group == lax.broadcasted_iota(jnp.int32, (ROWS, TOK), 1), 1.0, 0.0)
        vals = jnp.dot(spread.astype(BF16), valt_s[...], preferred_element_type=F32)
        pick = jnp.where(vals == (c - CAP * group).astype(F32), 1.0, 0.0).astype(BF16)
        rows_out = jnp.dot(pick, x_own, preferred_element_type=F32).astype(BF16)
        out_s[pl.ds(b * PER, PER)] = rows_out.reshape(PER, CAP, HD)

        @pl.loop(0, PER)
        def _(i):
            n = b * PER + i

            @pl.when(n == 0)
            def _():
                pltpu.make_async_copy(out_s.at[0], a_s.at[0], drecv.at[0]).start()

            @pl.when(n > 0)
            def _():
                pltpu.make_async_remote_copy(
                    src_ref=out_s.at[n],
                    dst_ref=a_s.at[n],
                    send_sem=dsend,
                    recv_sem=drecv.at[b],
                    device_id={"expert": chip_plus(me, n), "half": core},
                    device_id_type=MESH,
                ).start()

    @pl.loop(0, CHIPS)
    def _(n):
        mask_s[n] = jnp.full((CAP, 128), mod_ref[chip_minus(me, n), 0], jnp.int32).astype(F32)

    prow = lax.broadcasted_iota(jnp.int32, (256, 256), 0)
    pcol = lax.broadcasted_iota(jnp.int32, (256, 256), 1)
    part = jnp.where(pcol == jnp.where(prow < 128, 2 * prow, 2 * prow - 255), 1.0, 0.0).astype(BF16)
    loads[0].wait()

    @pl.loop(0, D // 128)
    def _(r):
        r0 = pl.multiple_of(r * 128, 128)
        for e in range(2):
            block = wraw[e, pl.ds(r0, 128)].reshape(256, UNITS)
            parted = jnp.dot(part, block, preferred_element_type=F32).astype(BF16)
            w_s[pl.ds(r0, 128), e * 2 * UNITS : e * 2 * UNITS + UNITS] = parted[:128]
            w_s[pl.ds(r0, 128), e * 2 * UNITS + UNITS : (e + 1) * 2 * UNITS] = parted[128:]

    loads[2].wait()

    @pl.loop(0, D // 128)
    def _(r):
        r0 = pl.multiple_of(r * 128, 128)
        block = kvraw[pl.ds(r0, 128)].reshape(256, 256)
        parted = jnp.dot(part, block, preferred_element_type=F32).astype(BF16)
        kvw_s[pl.ds(r0, 128), 0:256] = parted[:128]
        kvw_s[pl.ds(r0, 128), 256:512] = parted[128:]

    loads[1].wait()

    def pieces(ref, b):
        return ref.at[pl.ds(b * PER, PER)]

    def forward(b):
        pltpu.make_async_copy(pieces(a_s, b), pieces(a_s, b), drecv.at[b]).wait()
        pltpu.make_async_remote_copy(
            src_ref=pieces(a_s, b),
            dst_ref=pieces(b_s, b),
            send_sem=fsend.at[b],
            recv_sem=frecv.at[b],
            device_id={"expert": me, "half": mate},
            device_id_type=MESH,
        ).start()

    forward(0)

    @pl.loop(0, BATCHES)
    def _(b):
        pltpu.make_async_remote_copy(
            src_ref=pieces(a_s, b),
            dst_ref=pieces(b_s, b),
            send_sem=fsend.at[b],
            recv_sem=frecv.at[b],
            device_id={"expert": me, "half": mate},
            device_id_type=MESH,
        ).wait()
        xa = a_s[pl.ds(b * PER, PER)].reshape(ROWS, HD)
        xb = b_s[pl.ds(b * PER, PER)].reshape(ROWS, HD)

        @pl.loop(0, 4)
        def _(k):
            cols = pl.ds(pl.multiple_of(k * UNITS, 128), UNITS)
            gu_s[:, cols] = jnp.dot(
                xa, w_s[pl.ds(own, HD), cols], preferred_element_type=F32
            ) + jnp.dot(xb, w_s[pl.ds(oth, HD), cols], preferred_element_type=F32)

        mask = mask_s[pl.ds(b * PER, PER)].reshape(ROWS, 128)
        image = jnp.concatenate([mask, mask, mask], axis=1) > 0.5
        gate = jnp.where(image, gu_s[:, 2 * UNITS : 3 * UNITS], gu_s[:, :UNITS])
        up = jnp.where(image, gu_s[:, 3 * UNITS :], gu_s[:, UNITS : 2 * UNITS])
        act = gate / (1.0 + jnp.exp(-gate)) * up
        both = jnp.concatenate(
            [jnp.where(image, 0.0, act), jnp.where(image, act, 0.0)], axis=1
        ).astype(BF16)

        ps_s[...] = jnp.dot(both, wd_s[:, pl.ds(oth, HD)], preferred_element_type=F32)
        swap = pltpu.make_async_remote_copy(
            src_ref=ps_s,
            dst_ref=pr_s.at[b % 2],
            send_sem=psend,
            recv_sem=precv.at[b % 2],
            device_id={"expert": me, "half": mate},
            device_id_type=MESH,
        )
        swap.start()
        own_s[...] = jnp.dot(both, wd_s[:, pl.ds(own, HD)], preferred_element_type=F32)
        swap.wait()
        ret_s[pl.ds(b * PER, PER)] = (own_s[...] + pr_s[b % 2]).astype(BF16).reshape(PER, CAP, HD)

        @pl.loop(0, PER)
        def _(i):
            n = b * PER + i

            @pl.when(n == 0)
            def _():
                pltpu.make_async_copy(ret_s.at[0], rin_s.at[0], rrecv.at[0]).start()

            @pl.when(n > 0)
            def _():
                pltpu.make_async_remote_copy(
                    src_ref=ret_s.at[n],
                    dst_ref=rin_s.at[n],
                    send_sem=rsend,
                    recv_sem=rrecv.at[b],
                    device_id={"expert": chip_minus(me, n), "half": core},
                    device_id_type=MESH,
                ).start()

        @pl.when(b < BATCHES - 1)
        def _():
            forward(b + 1)

    acc_s[...] = x_ref[:, pl.ds(own, HD)].astype(F32)
    wide = 2 * ROWS

    @pl.loop(0, BATCHES // 2)
    def _(b):
        c = lax.broadcasted_iota(jnp.int32, (TOK, wide), 1) + b * wide
        group = slot_group(c)
        spread = jnp.where(group == lax.broadcasted_iota(jnp.int32, (TOK, wide), 0), 1.0, 0.0).astype(BF16)
        vals = jnp.dot(val_s[...], spread, preferred_element_type=F32)
        pick = vals == (c - CAP * group).astype(F32)
        w_hi = jnp.where(pick, jnp.dot(hi_s[...], spread, preferred_element_type=F32), 0.0).astype(BF16)
        w_lo = jnp.where(pick, jnp.dot(lo_s[...], spread, preferred_element_type=F32), 0.0).astype(BF16)
        for k in range(2):
            pltpu.make_async_copy(pieces(rin_s, 2 * b + k), pieces(rin_s, 2 * b + k), rrecv.at[2 * b + k]).wait()
        back = rin_s[pl.ds(b * 2 * PER, 2 * PER)].reshape(wide, HD)
        acc_s[...] += jnp.dot(w_hi, back, preferred_element_type=F32) + jnp.dot(
            w_lo, back, preferred_element_type=F32
        )

    ho_ref[:, pl.ds(own, HD)] = acc_s[...]
    share = pltpu.make_async_remote_copy(
        src_ref=acc_s,
        dst_ref=ho_ref.at[:, pl.ds(own, HD)],
        send_sem=hsend,
        recv_sem=hrecv,
        device_id={"expert": me, "half": mate},
        device_id_type=MESH,
    )
    share.start()
    loads[3].wait()
    share.wait()
    hidden = ho_ref[...]
    mean_sq = jnp.mean(hidden * hidden, axis=-1, keepdims=True)
    nrm_s[...] = (hidden * lax.rsqrt(mean_sq + EPSILON) * gain_ref[...]).astype(BF16)

    def head_norm(values, gain):
        scale = lax.rsqrt(jnp.mean(values * values, axis=-1, keepdims=True) + EPSILON)
        return (values * scale * gain).astype(BF16)

    @pl.loop(0, 4)
    def _(k):
        kv = jnp.dot(nrm_s[...], kvw_s[:, pl.ds(pl.multiple_of(k * 128, 128), 128)], preferred_element_type=F32)

        @pl.when(k < 2)
        def _():
            kv_ref[k] = head_norm(kv, kg_ref[...])

        @pl.when(k >= 2)
        def _():
            kv_ref[k] = kv.astype(BF16)

    @pl.loop(0, 8)
    def _(k):
        q2 = jnp.dot(nrm_s[...], wq_s[:, pl.ds(pl.multiple_of(k * 256, 256), 256)], preferred_element_type=F32)
        q_ref[2 * k] = head_norm(q2[:, :128], qg_ref[...])
        q_ref[2 * k + 1] = head_norm(q2[:, 128:], qg_ref[...])

    rest = pl.ds(1, CHIPS - 1)
    pltpu.make_async_copy(out_s.at[rest], out_s.at[rest], dsend).wait()
    pltpu.make_async_copy(ret_s.at[rest], ret_s.at[rest], rsend).wait()


def moe_call(x, mod, ids, rw, wgu, wd, gain, wq, wkv, qg, kg):
    vm = pl.BlockSpec(memory_space=pltpu.VMEM)
    hbm = pl.BlockSpec(memory_space=pl.ANY)
    sm = pl.BlockSpec(memory_space=pltpu.SMEM)
    dma = pltpu.SemaphoreType.DMA
    return pl.pallas_call(
        moe_kernel,
        out_shape=(
            jax.ShapeDtypeStruct((TOK, D), F32),
            jax.ShapeDtypeStruct((16, TOK, 128), BF16),
            jax.ShapeDtypeStruct((4, TOK, 128), BF16),
        ),
        in_specs=[vm, sm, vm, vm, hbm, hbm, vm, hbm, hbm, vm, vm],
        out_specs=(vm, vm, vm),
        scratch_shapes=[
            pltpu.VMEM((2, D, 2, UNITS), BF16),
            pltpu.VMEM((D, 4 * UNITS), BF16),
            pltpu.VMEM((2 * UNITS, D), BF16),
            pltpu.VMEM((D, D), BF16),
            pltpu.VMEM((D, 2, 256), BF16),
            pltpu.VMEM((D, 512), BF16),
            pltpu.VMEM((CHIPS, CAP, HD), BF16),
            pltpu.VMEM((CHIPS, CAP, HD), BF16),
            pltpu.VMEM((CHIPS, CAP, HD), BF16),
            pltpu.VMEM((CHIPS, CAP, HD), BF16),
            pltpu.VMEM((CHIPS, CAP, HD), BF16),
            pltpu.VMEM((ROWS, 4 * UNITS), F32),
            pltpu.VMEM((ROWS, HD), F32),
            pltpu.VMEM((ROWS, HD), F32),
            pltpu.VMEM((2, ROWS, HD), F32),
            pltpu.VMEM((CHIPS, CAP, 128), F32),
            pltpu.VMEM((TOK, TOK), BF16),
            pltpu.VMEM((TOK, TOK), BF16),
            pltpu.VMEM((TOK, TOK), BF16),
            pltpu.VMEM((TOK, TOK), BF16),
            pltpu.VMEM((TOK, HD), F32),
            pltpu.VMEM((TOK, D), BF16),
            dma((4,)),
            dma,
            dma((BATCHES,)),
            dma((BATCHES,)),
            dma((BATCHES,)),
            dma,
            dma((2,)),
            dma,
            dma((BATCHES,)),
            dma,
            dma,
        ],
        compiler_params=pltpu.CompilerParams(
            collective_id=0, has_side_effects=True, vmem_limit_bytes=62 * 1024 * 1024
        ),
    )(x, mod, ids, rw, wgu, wd, gain, wq, wkv, qg, kg)


LOG2E = 1.4426950408889634
PARTS = (((2, 0, 1), 48, 0), ((0, 1, 2), 40, 48), ((1, 2, 0), 40, 88))
QCOLS = 512
KEYS = 2048
UNITS_KV = 4
VROWS = 144


def group_shift(k):
    return k + k // 2 - 2 * (k // 3)


def attention_kernel(
    q_ref, kv_ref, o_ref, buf0, buf1, buf2, kun, vun, vt_s, s0, s1, m_s, acc_s, ssem, rsem
):
    me = lax.axis_index("expert")
    core = lax.axis_index("half")
    place = (me // 16, (me // 4) % 4, me % 4)
    bufs = (buf0, buf1, buf2)

    def neighbour(axis, step):
        moved = [(place[i] + (step if i == axis else 0)) % 4 for i in range(3)]
        return {"expert": moved[0] * 16 + moved[1] * 4 + moved[2], "half": core}

    barrier = pltpu.get_barrier_semaphore()
    for axis in range(3):
        for step in (1, 3):
            pl.semaphore_signal(barrier, inc=1, device_id=neighbour(axis, step), device_id_type=MESH)
    spots = []
    for p, (axes, rows, first) in enumerate(PARTS):
        a, b, c = (place[i] for i in axes)
        spots.append((a, b, c))
        for kind in range(4):
            bufs[p][c, kind, b, a] = kv_ref[kind, first : first + rows, :]
    m_s[...] = jnp.full_like(m_s, -1e30)
    acc_s[...] = jnp.zeros_like(acc_s)
    vt_s[:, 128:, :] = jnp.ones((2, VROWS - 128, KEYS), BF16)
    pl.semaphore_wait(barrier, 6)

    def send(p, view, phase, step, mark):
        pltpu.make_async_remote_copy(
            src_ref=view,
            dst_ref=view,
            send_sem=ssem.at[p, phase],
            recv_sem=rsem.at[p, mark],
            device_id=neighbour(PARTS[p][0][phase], step),
            device_id_type=MESH,
        ).start()

    def landed(p, view, mark):
        pltpu.make_async_copy(view, view, rsem.at[p, mark]).wait()

    early, late, every = pl.ds(0, 2), pl.ds(2, 2), pl.ds(0, 4)

    def one(p, shift, kinds):
        a, b, c = spots[p]
        return bufs[p].at[c, kinds, b, (a + shift) % 4]

    def line(p, shift, kinds):
        a, b, c = spots[p]
        return bufs[p].at[c, kinds, (b + shift) % 4]

    def sheet(p, shift, k, kinds):
        a, b, c = spots[p]
        return bufs[p].at[(c + shift) % 4, kinds, (b + group_shift(k)) % 4]

    def ring(view, phase, base):
        for p in range(3):
            send(p, view(p, 0, every), phase, 1, base)
            send(p, view(p, 0, every), phase, 3, base + 1)

    def pass_on(view, phase, base):
        for p in range(3):
            landed(p, view(p, 3, every), base)
            landed(p, view(p, 1, every), base + 1)
            send(p, view(p, 3, early), phase, 1, base + 2)
            send(p, view(p, 1, late), phase, 3, base + 3)

    def opposite(view, base):
        for p in range(3):
            landed(p, view(p, 2, early), base + 2)
            landed(p, view(p, 2, late), base + 3)

    def group(k):
        return lambda p, shift, kinds: sheet(p, shift, k, kinds)

    ring(one, 0, 0)
    pass_on(one, 0, 0)
    opposite(one, 0)
    ring(line, 1, 4)
    ring(group(0), 2, 8)
    pass_on(line, 1, 4)
    ring(group(1), 2, 12)
    ring(group(2), 2, 16)
    opposite(line, 4)
    ring(group(3), 2, 20)

    scale = 128**-0.5 * LOG2E

    def scores(h, r):
        cols = pl.ds(pl.multiple_of(r * QCOLS, QCOLS), QCOLS)
        return lax.dot_general(kun[h], q_ref[h, cols], (((1,), (1,)), ((), ())), preferred_element_type=F32)

    def absorb(h, s_ref, r):
        cols = pl.ds(pl.multiple_of(r * QCOLS, QCOLS), QCOLS)
        s = s_ref[...]
        m_old = m_s[h, :, cols]
        m_new = jnp.maximum(m_old, jnp.max(s, axis=0, keepdims=True))
        m_s[h, :, cols] = m_new
        probs = jnp.exp2(s * scale - m_new * scale).astype(BF16)
        fade = jnp.exp2((m_old - m_new) * scale)
        acc_s[h, :, cols] = acc_s[h, :, cols] * fade + jnp.dot(vt_s[h], probs, preferred_element_type=F32)

    steps = q_ref.shape[1] // QCOLS

    @pl.loop(0, UNITS_KV)
    def _(u):
        @pl.when(u == 1)
        def _():
            pass_on(group(0), 2, 8)
            pass_on(group(1), 2, 12)

        @pl.when(u == 2)
        def _():
            pass_on(group(2), 2, 16)
            pass_on(group(3), 2, 20)

        @pl.when(u == 3)
        def _():
            for k in range(4):
                opposite(group(k), 8 + 4 * k)

        mid = (u % 3 + 1) // 2
        start = 0
        for p, (axes, rows, first) in enumerate(PARTS):
            a, b, c = spots[p]
            for i in range(4):
                shift_c = (1 - mid) * 2 * (u // 3) + mid * (3 - 2 * (i // 2))
                k = (1 - mid) * i + mid * (2 * (u - 1) + i % 2)
                at_c, at_b = (c + shift_c) % 4, (b + group_shift(k)) % 4
                for h in range(2):
                    kun[h, start : start + 4 * rows] = bufs[p][at_c, h, at_b].reshape(4 * rows, 128)
                    vun[h, start : start + 4 * rows] = bufs[p][at_c, 2 + h, at_b].reshape(4 * rows, 128)
                start += 4 * rows
        for h in range(2):
            vt_s[h, :128, :] = vun[h].T

        s0[...] = scores(0, 0)

        @pl.loop(0, steps)
        def _(r):
            s1[...] = scores(1, r)
            absorb(0, s0, r)
            s0[...] = scores(0, lax.rem(r + 1, steps))
            absorb(1, s1, r)

    for h in range(2):
        for j in range(8):
            cols = slice(j * 128, (j + 1) * 128)
            head = acc_s[h, :128, cols] / acc_s[h, 128:129, cols]
            o_ref[:, (h * 8 + j) * 128 : (h * 8 + j + 1) * 128] = head.T.astype(BF16)

    three = pl.ds(0, 3)
    for p in range(3):
        a, b, c = spots[p]
        view = bufs[p].at[c, :, b, three]
        pltpu.make_async_copy(view, view, ssem.at[p, 0]).wait()
        view = bufs[p].at[c, :, three]
        pltpu.make_async_copy(view, view, ssem.at[p, 1]).wait()
        view = bufs[p].at[three]
        pltpu.make_async_copy(view, view, ssem.at[p, 2]).wait()


def attention_call(queries, kv_block):
    vm = pl.BlockSpec(memory_space=pltpu.VMEM)
    dma = pltpu.SemaphoreType.DMA
    return pl.pallas_call(
        attention_kernel,
        out_shape=jax.ShapeDtypeStruct((TOK, D), BF16),
        in_specs=[vm, vm],
        out_specs=vm,
        scratch_shapes=[pltpu.VMEM((4, 4, 4, 4, rows, 128), BF16) for _, rows, _ in PARTS]
        + [
            pltpu.VMEM((2, KEYS, 128), BF16),
            pltpu.VMEM((2, KEYS, 128), BF16),
            pltpu.VMEM((2, VROWS, KEYS), BF16),
            pltpu.VMEM((KEYS, QCOLS), F32),
            pltpu.VMEM((KEYS, QCOLS), F32),
            pltpu.VMEM((2, 1, 1024), F32),
            pltpu.VMEM((2, VROWS, 1024), F32),
            dma((3, 3)),
            dma((3, 24)),
        ],
        compiler_params=pltpu.CompilerParams(
            collective_id=1, has_side_effects=True, vmem_limit_bytes=48 * 1024 * 1024
        ),
    )(queries, kv_block)


def body(hidden_in, modality, expert_ids, route_weights, w_gate_up, w_down, norm_gain, w_query,
         key_value_weight, q_gain, k_gain):
    hidden_out, queries, kv_block = moe_call(
        hidden_in, modality.reshape(CHIPS, TOK), expert_ids, route_weights, w_gate_up,
        w_down.reshape(2 * UNITS, D), norm_gain.reshape(1, D), w_query, key_value_weight,
        q_gain.reshape(1, 128), k_gain.reshape(1, 128),
    )
    attended = attention_call(queries.reshape(2, 8 * TOK, 128), kv_block)
    return hidden_out, attended


def solution(mesh):
    in_specs = (
        P("expert", None), P(), P("expert", None), P("expert", None),
        P("expert", None, None, "half"), P("expert", "half", None), P(), P(None, "half"),
        P(None, None, "half"), P(), P(),
    )
    out_specs = (P("expert", None), P("expert", "half"))
    return jax.shard_map(body, mesh=mesh, in_specs=in_specs, out_specs=out_specs, check_vma=False)
```

```python
import functools
import jax
import jax.numpy as jnp
from jax import lax
from jax.experimental import pallas as pl
from jax.experimental.pallas import tpu as pltpu
from jax.sharding import PartitionSpec as P

EPSILON = 1e-06
MESH = pl.DeviceIdType.MESH
F32 = jnp.float32
BF16 = jnp.bfloat16

CHIPS = 64
CAP = 24
TOK = 128
D = 2048
HD = 1024
UNITS = 384
PER = 8
BATCHES = CHIPS // PER
ROWS = PER * CAP
AHEAD = 4


def offsets(n):
    a, b, c = n // 16, (n // 4) % 4, n % 4
    return c, (c + b) % 4, (c + a) % 4


def chip_plus(chip, n):
    oy, oz, ox = offsets(n)
    y, z, x = chip // 16, (chip // 4) % 4, chip % 4
    return ((y + oy) % 4) * 16 + ((z + oz) % 4) * 4 + (x + ox) % 4


def chip_minus(chip, n):
    oy, oz, ox = offsets(n)
    y, z, x = chip // 16, (chip // 4) % 4, chip % 4
    return ((y + 4 - oy) % 4) * 16 + ((z + 4 - oz) % 4) * 4 + (x + 4 - ox) % 4


def slot_group(c):
    return (c * 2731) >> 16


def moe_kernel(
    x_ref, mod_ref, ids_ref, rw_ref, wgu_hbm, wd_hbm, gain_ref, wq_hbm, wkv_hbm, qg_ref, kg_ref,
    ho_ref, q_ref, kv_ref,
    wraw, w_s, wd_s, wq_s, kvraw, kvw_s, out_s, a_s, b_s, ret_s, rin_s, gu_s, own_s, ps_s, pr_s,
    mask_s, val_s, hi_s, lo_s, valt_s, acc_s, nrm_s,
    wsem, dsend, drecv, fsend, frecv, psend, precv, rsend, rrecv, hsend, hrecv,
):
    me = lax.axis_index("expert")
    core = lax.axis_index("half")
    mate = 1 - core
    own = pl.multiple_of(core * HD, HD)
    oth = pl.multiple_of(mate * HD, HD)

    loads = [
        pltpu.make_async_copy(wgu_hbm, wraw, wsem.at[0]),
        pltpu.make_async_copy(wd_hbm, wd_s, wsem.at[1]),
        pltpu.make_async_copy(wkv_hbm, kvraw, wsem.at[2]),
        pltpu.make_async_copy(wq_hbm, wq_s, wsem.at[3]),
    ]
    for load in loads:
        load.start()

    barrier = pltpu.get_barrier_semaphore()
    pl.semaphore_signal(barrier, inc=1, device_id={"expert": me, "half": mate}, device_id_type=MESH)

    @pl.loop(1, CHIPS)
    def _(n):
        pl.semaphore_signal(
            barrier, inc=1, device_id={"expert": chip_plus(me, n), "half": core}, device_id_type=MESH
        )

    row = lax.broadcasted_iota(jnp.int32, (TOK, TOK), 0)
    lane = lax.broadcasted_iota(jnp.int32, (TOK, TOK), 1)
    ra, rb, rc = row >> 4, (row >> 2) & 3, row & 3
    my_y, my_z, my_x = me // 16, (me // 4) % 4, me % 4
    target = ((my_y + rc) & 3) * 16 + ((my_z + rc + rb) & 3) * 4 + ((my_x + rc + ra) & 3)
    target = jnp.where(row < CHIPS, target, -1)
    member = jnp.zeros((TOK, TOK), F32)
    weight = jnp.zeros((TOK, TOK), F32)
    for j in range(ids_ref.shape[0]):
        hit = jnp.broadcast_to(ids_ref[j : j + 1, :], (TOK, TOK)) == target
        member = member + jnp.where(hit, 1.0, 0.0)
        weight = weight + jnp.where(hit, jnp.broadcast_to(rw_ref[j : j + 1, :], (TOK, TOK)), 0.0)
    earlier = jnp.where(row < lane, 1.0, 0.0).astype(BF16)
    rank = jnp.dot(member.astype(BF16), earlier, preferred_element_type=F32)
    val = jnp.where(member > 0.5, rank, -1.0)
    valt_s[...] = val.astype(BF16)
    val_s[...] = val.T.astype(BF16)
    weight = weight.T
    high = weight.astype(BF16)
    hi_s[...] = high
    lo_s[...] = (weight - high.astype(F32)).astype(BF16)

    pl.semaphore_wait(barrier, CHIPS)

    def dispatch(b):
        @pl.loop(0, PER)
        def _(i):
            n = b * PER + i

            @pl.when(n == 0)
            def _():
                pltpu.make_async_copy(out_s.at[0], a_s.at[0], drecv.at[0]).start()

            @pl.when(n > 0)
            def _():
                pltpu.make_async_remote_copy(
                    src_ref=out_s.at[n],
                    dst_ref=a_s.at[n],
                    send_sem=dsend,
                    recv_sem=drecv.at[b],
                    device_id={"expert": chip_plus(me, n), "half": core},
                    device_id_type=MESH,
                ).start()

    x_own = x_ref[:, pl.ds(own, HD)]

    @pl.loop(0, BATCHES)
    def _(b):
        c = lax.broadcasted_iota(jnp.int32, (ROWS, TOK), 0) + b * ROWS
        group = slot_group(c)
        spread = jnp.where(group == lax.broadcasted_iota(jnp.int32, (ROWS, TOK), 1), 1.0, 0.0)
        vals = jnp.dot(spread.astype(BF16), valt_s[...], preferred_element_type=F32)
        pick = jnp.where(vals == (c - CAP * group).astype(F32), 1.0, 0.0).astype(BF16)
        rows_out = jnp.dot(pick, x_own, preferred_element_type=F32).astype(BF16)
        out_s[pl.ds(b * PER, PER)] = rows_out.reshape(PER, CAP, HD)

        @pl.when(b < AHEAD)
        def _():
            dispatch(b)

    @pl.loop(0, CHIPS)
    def _(n):
        mask_s[n] = jnp.full((CAP, 128), mod_ref[chip_minus(me, n), 0], jnp.int32).astype(F32)

    prow = lax.broadcasted_iota(jnp.int32, (256, 256), 0)
    pcol = lax.broadcasted_iota(jnp.int32, (256, 256), 1)
    part = jnp.where(pcol == jnp.where(prow < 128, 2 * prow, 2 * prow - 255), 1.0, 0.0).astype(BF16)
    loads[0].wait()

    @pl.loop(0, D // 128)
    def _(r):
        r0 = pl.multiple_of(r * 128, 128)
        for e in range(2):
            block = wraw[e, pl.ds(r0, 128)].reshape(256, UNITS)
            parted = jnp.dot(part, block, preferred_element_type=F32).astype(BF16)
            w_s[pl.ds(r0, 128), e * 2 * UNITS : e * 2 * UNITS + UNITS] = parted[:128]
            w_s[pl.ds(r0, 128), e * 2 * UNITS + UNITS : (e + 1) * 2 * UNITS] = parted[128:]

    loads[2].wait()

    @pl.loop(0, D // 128)
    def _(r):
        r0 = pl.multiple_of(r * 128, 128)
        block = kvraw[pl.ds(r0, 128)].reshape(256, 256)
        parted = jnp.dot(part, block, preferred_element_type=F32).astype(BF16)
        kvw_s[pl.ds(r0, 128), 0:256] = parted[:128]
        kvw_s[pl.ds(r0, 128), 256:512] = parted[128:]

    loads[1].wait()

    def pieces(ref, b):
        return ref.at[pl.ds(b * PER, PER)]

    def forward(b):
        pltpu.make_async_copy(pieces(a_s, b), pieces(a_s, b), drecv.at[b]).wait()
        pltpu.make_async_remote_copy(
            src_ref=pieces(a_s, b),
            dst_ref=pieces(b_s, b),
            send_sem=fsend.at[b],
            recv_sem=frecv.at[b],
            device_id={"expert": me, "half": mate},
            device_id_type=MESH,
        ).start()

    forward(0)

    @pl.loop(0, BATCHES)
    def _(b):
        pltpu.make_async_remote_copy(
            src_ref=pieces(a_s, b),
            dst_ref=pieces(b_s, b),
            send_sem=fsend.at[b],
            recv_sem=frecv.at[b],
            device_id={"expert": me, "half": mate},
            device_id_type=MESH,
        ).wait()
        xa = a_s[pl.ds(b * PER, PER)].reshape(ROWS, HD)
        xb = b_s[pl.ds(b * PER, PER)].reshape(ROWS, HD)

        @pl.loop(0, 4)
        def _(k):
            cols = pl.ds(pl.multiple_of(k * UNITS, 128), UNITS)
            gu_s[:, cols] = jnp.dot(
                xa, w_s[pl.ds(own, HD), cols], preferred_element_type=F32
            ) + jnp.dot(xb, w_s[pl.ds(oth, HD), cols], preferred_element_type=F32)

        mask = mask_s[pl.ds(b * PER, PER)].reshape(ROWS, 128)
        image = jnp.concatenate([mask, mask, mask], axis=1) > 0.5
        gate = jnp.where(image, gu_s[:, 2 * UNITS : 3 * UNITS], gu_s[:, :UNITS])
        up = jnp.where(image, gu_s[:, 3 * UNITS :], gu_s[:, UNITS : 2 * UNITS])
        act = gate / (1.0 + jnp.exp(-gate)) * up
        both = jnp.concatenate(
            [jnp.where(image, 0.0, act), jnp.where(image, act, 0.0)], axis=1
        ).astype(BF16)

        ps_s[...] = jnp.dot(both, wd_s[:, pl.ds(oth, HD)], preferred_element_type=F32)
        swap = pltpu.make_async_remote_copy(
            src_ref=ps_s,
            dst_ref=pr_s.at[b % 2],
            send_sem=psend,
            recv_sem=precv.at[b % 2],
            device_id={"expert": me, "half": mate},
            device_id_type=MESH,
        )
        swap.start()
        own_s[...] = jnp.dot(both, wd_s[:, pl.ds(own, HD)], preferred_element_type=F32)
        swap.wait()
        ret_s[pl.ds(b * PER, PER)] = (own_s[...] + pr_s[b % 2]).astype(BF16).reshape(PER, CAP, HD)

        @pl.loop(0, PER)
        def _(i):
            n = b * PER + i

            @pl.when(n == 0)
            def _():
                pltpu.make_async_copy(ret_s.at[0], rin_s.at[0], rrecv.at[0]).start()

            @pl.when(n > 0)
            def _():
                pltpu.make_async_remote_copy(
                    src_ref=ret_s.at[n],
                    dst_ref=rin_s.at[n],
                    send_sem=rsend,
                    recv_sem=rrecv.at[b],
                    device_id={"expert": chip_minus(me, n), "half": core},
                    device_id_type=MESH,
                ).start()

        @pl.when(b + AHEAD < BATCHES)
        def _():
            dispatch(b + AHEAD)

        @pl.when(b < BATCHES - 1)
        def _():
            forward(b + 1)

    acc_s[...] = x_ref[:, pl.ds(own, HD)].astype(F32)
    wide = 2 * ROWS

    @pl.loop(0, BATCHES // 2)
    def _(b):
        c = lax.broadcasted_iota(jnp.int32, (TOK, wide), 1) + b * wide
        group = slot_group(c)
        spread = jnp.where(group == lax.broadcasted_iota(jnp.int32, (TOK, wide), 0), 1.0, 0.0).astype(BF16)
        vals = jnp.dot(val_s[...], spread, preferred_element_type=F32)
        pick = vals == (c - CAP * group).astype(F32)
        w_hi = jnp.where(pick, jnp.dot(hi_s[...], spread, preferred_element_type=F32), 0.0).astype(BF16)
        w_lo = jnp.where(pick, jnp.dot(lo_s[...], spread, preferred_element_type=F32), 0.0).astype(BF16)
        for k in range(2):
            pltpu.make_async_copy(pieces(rin_s, 2 * b + k), pieces(rin_s, 2 * b + k), rrecv.at[2 * b + k]).wait()
        back = rin_s[pl.ds(b * 2 * PER, 2 * PER)].reshape(wide, HD)
        acc_s[...] += jnp.dot(w_hi, back, preferred_element_type=F32) + jnp.dot(
            w_lo, back, preferred_element_type=F32
        )

    ho_ref[:, pl.ds(own, HD)] = acc_s[...]
    share = pltpu.make_async_remote_copy(
        src_ref=acc_s,
        dst_ref=ho_ref.at[:, pl.ds(own, HD)],
        send_sem=hsend,
        recv_sem=hrecv,
        device_id={"expert": me, "half": mate},
        device_id_type=MESH,
    )
    share.start()
    loads[3].wait()
    share.wait()
    hidden = ho_ref[...]
    mean_sq = jnp.mean(hidden * hidden, axis=-1, keepdims=True)
    nrm_s[...] = (hidden * lax.rsqrt(mean_sq + EPSILON) * gain_ref[...]).astype(BF16)

    def head_norm(values, gain):
        scale = lax.rsqrt(jnp.mean(values * values, axis=-1, keepdims=True) + EPSILON)
        return (values * scale * gain).astype(BF16)

    @pl.loop(0, 4)
    def _(k):
        kv = jnp.dot(nrm_s[...], kvw_s[:, pl.ds(pl.multiple_of(k * 128, 128), 128)], preferred_element_type=F32)

        @pl.when(k < 2)
        def _():
            kv_ref[k] = head_norm(kv, kg_ref[...])

        @pl.when(k >= 2)
        def _():
            kv_ref[k] = kv.astype(BF16)

    @pl.loop(0, 8)
    def _(k):
        q2 = jnp.dot(nrm_s[...], wq_s[:, pl.ds(pl.multiple_of(k * 256, 256), 256)], preferred_element_type=F32)
        q_ref[2 * k] = head_norm(q2[:, :128], qg_ref[...])
        q_ref[2 * k + 1] = head_norm(q2[:, 128:], qg_ref[...])

    rest = pl.ds(1, CHIPS - 1)
    pltpu.make_async_copy(out_s.at[rest], out_s.at[rest], dsend).wait()
    pltpu.make_async_copy(ret_s.at[rest], ret_s.at[rest], rsend).wait()


def moe_call(x, mod, ids, rw, wgu, wd, gain, wq, wkv, qg, kg):
    vm = pl.BlockSpec(memory_space=pltpu.VMEM)
    hbm = pl.BlockSpec(memory_space=pl.ANY)
    sm = pl.BlockSpec(memory_space=pltpu.SMEM)
    dma = pltpu.SemaphoreType.DMA
    return pl.pallas_call(
        moe_kernel,
        out_shape=(
            jax.ShapeDtypeStruct((TOK, D), F32),
            jax.ShapeDtypeStruct((16, TOK, 128), BF16),
            jax.ShapeDtypeStruct((4, TOK, 128), BF16),
        ),
        in_specs=[vm, sm, vm, vm, hbm, hbm, vm, hbm, hbm, vm, vm],
        out_specs=(vm, vm, vm),
        scratch_shapes=[
            pltpu.VMEM((2, D, 2, UNITS), BF16),
            pltpu.VMEM((D, 4 * UNITS), BF16),
            pltpu.VMEM((2 * UNITS, D), BF16),
            pltpu.VMEM((D, D), BF16),
            pltpu.VMEM((D, 2, 256), BF16),
            pltpu.VMEM((D, 512), BF16),
            pltpu.VMEM((CHIPS, CAP, HD), BF16),
            pltpu.VMEM((CHIPS, CAP, HD), BF16),
            pltpu.VMEM((CHIPS, CAP, HD), BF16),
            pltpu.VMEM((CHIPS, CAP, HD), BF16),
            pltpu.VMEM((CHIPS, CAP, HD), BF16),
            pltpu.VMEM((ROWS, 4 * UNITS), F32),
            pltpu.VMEM((ROWS, HD), F32),
            pltpu.VMEM((ROWS, HD), F32),
            pltpu.VMEM((2, ROWS, HD), F32),
            pltpu.VMEM((CHIPS, CAP, 128), F32),
            pltpu.VMEM((TOK, TOK), BF16),
            pltpu.VMEM((TOK, TOK), BF16),
            pltpu.VMEM((TOK, TOK), BF16),
            pltpu.VMEM((TOK, TOK), BF16),
            pltpu.VMEM((TOK, HD), F32),
            pltpu.VMEM((TOK, D), BF16),
            dma((4,)),
            dma,
            dma((BATCHES,)),
            dma((BATCHES,)),
            dma((BATCHES,)),
            dma,
            dma((2,)),
            dma,
            dma((BATCHES,)),
            dma,
            dma,
        ],
        compiler_params=pltpu.CompilerParams(
            collective_id=0, has_side_effects=True, vmem_limit_bytes=62 * 1024 * 1024
        ),
    )(x, mod, ids, rw, wgu, wd, gain, wq, wkv, qg, kg)


LOG2E = 1.4426950408889634
PARTS = (((2, 0, 1), 48, 0), ((0, 1, 2), 40, 48), ((1, 2, 0), 40, 88))
QCOLS = 512
KEYS = 2048
UNITS_KV = 4
VROWS = 144


def group_shift(k):
    return k + k // 2 - 2 * (k // 3)


def attention_kernel(
    q_ref, kv_ref, o_ref, buf0, buf1, buf2, kun, vun, vt_s, s0, s1, m_s, acc_s, ssem, rsem
):
    me = lax.axis_index("expert")
    core = lax.axis_index("half")
    place = (me // 16, (me // 4) % 4, me % 4)
    bufs = (buf0, buf1, buf2)

    def along(i, axis):
        return 1 - ((i + 6 - axis - core) % 3 + 1) // 2

    def coordinate(axis):
        return sum(place[i] * along(i, axis) for i in range(3))

    def neighbour(axis, step):
        moved = [(place[i] + step * along(i, axis)) % 4 for i in range(3)]
        return {"expert": moved[0] * 16 + moved[1] * 4 + moved[2], "half": core}

    barrier = pltpu.get_barrier_semaphore()
    for axis in range(3):
        for step in (1, 3):
            pl.semaphore_signal(barrier, inc=1, device_id=neighbour(axis, step), device_id_type=MESH)
    spots = []
    for p, (axes, rows, first) in enumerate(PARTS):
        a, b, c = (coordinate(axis) for axis in axes)
        spots.append((a, b, c))
        for kind in range(4):
            bufs[p][c, kind, b, a] = kv_ref[kind, first : first + rows, :]
    m_s[...] = jnp.full_like(m_s, -1e30)
    acc_s[...] = jnp.zeros_like(acc_s)
    vt_s[:, 128:, :] = jnp.ones((2, VROWS - 128, KEYS), BF16)
    pl.semaphore_wait(barrier, 6)

    def send(p, view, phase, step, mark):
        pltpu.make_async_remote_copy(
            src_ref=view,
            dst_ref=view,
            send_sem=ssem.at[p, phase],
            recv_sem=rsem.at[p, mark],
            device_id=neighbour(PARTS[p][0][phase], step),
            device_id_type=MESH,
        ).start()

    def landed(p, view, mark):
        pltpu.make_async_copy(view, view, rsem.at[p, mark]).wait()

    early, late, every = pl.ds(0, 2), pl.ds(2, 2), pl.ds(0, 4)

    def one(p, shift, kinds):
        a, b, c = spots[p]
        return bufs[p].at[c, kinds, b, (a + shift) % 4]

    def line(p, shift, kinds):
        a, b, c = spots[p]
        return bufs[p].at[c, kinds, (b + shift) % 4]

    def sheet(p, shift, k, kinds):
        a, b, c = spots[p]
        return bufs[p].at[(c + shift) % 4, kinds, (b + group_shift(k)) % 4]

    def ring(view, phase, base):
        for p in range(3):
            send(p, view(p, 0, every), phase, 1, base)
            send(p, view(p, 0, every), phase, 3, base + 1)

    def pass_on(view, phase, base):
        for p in range(3):
            landed(p, view(p, 3, every), base)
            landed(p, view(p, 1, every), base + 1)
            send(p, view(p, 3, early), phase, 1, base + 2)
            send(p, view(p, 1, late), phase, 3, base + 3)

    def opposite(view, base):
        for p in range(3):
            landed(p, view(p, 2, early), base + 2)
            landed(p, view(p, 2, late), base + 3)

    def group(k):
        return lambda p, shift, kinds: sheet(p, shift, k, kinds)

    ring(one, 0, 0)
    pass_on(one, 0, 0)
    opposite(one, 0)
    ring(line, 1, 4)
    ring(group(0), 2, 8)
    pass_on(line, 1, 4)
    ring(group(1), 2, 12)
    ring(group(2), 2, 16)
    opposite(line, 4)
    ring(group(3), 2, 20)

    scale = 128**-0.5 * LOG2E

    def scores(h, r):
        cols = pl.ds(pl.multiple_of(r * QCOLS, QCOLS), QCOLS)
        return lax.dot_general(kun[h], q_ref[h, cols], (((1,), (1,)), ((), ())), preferred_element_type=F32)

    def absorb(h, s_ref, r):
        cols = pl.ds(pl.multiple_of(r * QCOLS, QCOLS), QCOLS)
        s = s_ref[...]
        m_old = m_s[h, :, cols]
        m_new = jnp.maximum(m_old, jnp.max(s, axis=0, keepdims=True))
        m_s[h, :, cols] = m_new
        probs = jnp.exp2(s * scale - m_new * scale).astype(BF16)
        fade = jnp.exp2((m_old - m_new) * scale)
        acc_s[h, :, cols] = acc_s[h, :, cols] * fade + jnp.dot(vt_s[h], probs, preferred_element_type=F32)

    steps = q_ref.shape[1] // QCOLS

    @pl.loop(0, UNITS_KV)
    def _(u):
        @pl.when(u == 1)
        def _():
            pass_on(group(0), 2, 8)
            pass_on(group(1), 2, 12)

        @pl.when(u == 2)
        def _():
            pass_on(group(2), 2, 16)
            pass_on(group(3), 2, 20)

        @pl.when(u == 3)
        def _():
            for k in range(4):
                opposite(group(k), 8 + 4 * k)

        mid = (u % 3 + 1) // 2
        start = 0
        for p, (axes, rows, first) in enumerate(PARTS):
            a, b, c = spots[p]
            for i in range(4):
                shift_c = (1 - mid) * 2 * (u // 3) + mid * (3 - 2 * (i // 2))
                k = (1 - mid) * i + mid * (2 * (u - 1) + i % 2)
                at_c, at_b = (c + shift_c) % 4, (b + group_shift(k)) % 4
                for h in range(2):
                    kun[h, start : start + 4 * rows] = bufs[p][at_c, h, at_b].reshape(4 * rows, 128)
                    vun[h, start : start + 4 * rows] = bufs[p][at_c, 2 + h, at_b].reshape(4 * rows, 128)
                start += 4 * rows
        for h in range(2):
            vt_s[h, :128, :] = vun[h].T

        s0[...] = scores(0, 0)

        @pl.loop(0, steps)
        def _(r):
            s1[...] = scores(1, r)
            absorb(0, s0, r)
            s0[...] = scores(0, lax.rem(r + 1, steps))
            absorb(1, s1, r)

    for h in range(2):
        for j in range(8):
            cols = slice(j * 128, (j + 1) * 128)
            head = acc_s[h, :128, cols] / acc_s[h, 128:129, cols]
            o_ref[:, (h * 8 + j) * 128 : (h * 8 + j + 1) * 128] = head.T.astype(BF16)

    three = pl.ds(0, 3)
    for p in range(3):
        a, b, c = spots[p]
        view = bufs[p].at[c, :, b, three]
        pltpu.make_async_copy(view, view, ssem.at[p, 0]).wait()
        view = bufs[p].at[c, :, three]
        pltpu.make_async_copy(view, view, ssem.at[p, 1]).wait()
        view = bufs[p].at[three]
        pltpu.make_async_copy(view, view, ssem.at[p, 2]).wait()


def attention_call(queries, kv_block):
    vm = pl.BlockSpec(memory_space=pltpu.VMEM)
    dma = pltpu.SemaphoreType.DMA
    return pl.pallas_call(
        attention_kernel,
        out_shape=jax.ShapeDtypeStruct((TOK, D), BF16),
        in_specs=[vm, vm],
        out_specs=vm,
        scratch_shapes=[pltpu.VMEM((4, 4, 4, 4, rows, 128), BF16) for _, rows, _ in PARTS]
        + [
            pltpu.VMEM((2, KEYS, 128), BF16),
            pltpu.VMEM((2, KEYS, 128), BF16),
            pltpu.VMEM((2, VROWS, KEYS), BF16),
            pltpu.VMEM((KEYS, QCOLS), F32),
            pltpu.VMEM((KEYS, QCOLS), F32),
            pltpu.VMEM((2, 1, 1024), F32),
            pltpu.VMEM((2, VROWS, 1024), F32),
            dma((3, 3)),
            dma((3, 24)),
        ],
        compiler_params=pltpu.CompilerParams(
            collective_id=1, has_side_effects=True, vmem_limit_bytes=48 * 1024 * 1024
        ),
    )(queries, kv_block)


def body(hidden_in, modality, expert_ids, route_weights, w_gate_up, w_down, norm_gain, w_query,
         key_value_weight, q_gain, k_gain):
    hidden_out, queries, kv_block = moe_call(
        hidden_in, modality.reshape(CHIPS, TOK), expert_ids.T, route_weights.T, w_gate_up,
        w_down.reshape(2 * UNITS, D), norm_gain.reshape(1, D), w_query, key_value_weight,
        q_gain.reshape(1, 128), k_gain.reshape(1, 128),
    )
    attended = attention_call(queries.reshape(2, 8 * TOK, 128), kv_block)
    return hidden_out, attended


def solution(mesh):
    in_specs = (
        P("expert", None), P(), P("expert", None), P("expert", None),
        P("expert", None, None, "half"), P("expert", "half", None), P(), P(None, "half"),
        P(None, None, "half"), P(), P(),
    )
    out_specs = (P("expert", None), P("expert", "half"))
    return jax.shard_map(body, mesh=mesh, in_specs=in_specs, out_specs=out_specs, check_vma=False)
```

```python
import functools
import jax
import jax.numpy as jnp
from jax import lax
from jax.experimental import pallas as pl
from jax.experimental.pallas import tpu as pltpu
from jax.sharding import PartitionSpec as P

EPSILON = 1e-06
MESH = pl.DeviceIdType.MESH
F32 = jnp.float32
BF16 = jnp.bfloat16

CHIPS = 64
CAP = 24
TOK = 128
D = 2048
HD = 1024
UNITS = 384
PER = 8
BATCHES = CHIPS // PER
ROWS = PER * CAP
AHEAD = 4


def offsets(n):
    a, b, c = n // 16, (n // 4) % 4, n % 4
    return c, (c + b) % 4, (c + a) % 4


def chip_plus(chip, n):
    oy, oz, ox = offsets(n)
    y, z, x = chip // 16, (chip // 4) % 4, chip % 4
    return ((y + oy) % 4) * 16 + ((z + oz) % 4) * 4 + (x + ox) % 4


def chip_minus(chip, n):
    oy, oz, ox = offsets(n)
    y, z, x = chip // 16, (chip // 4) % 4, chip % 4
    return ((y + 4 - oy) % 4) * 16 + ((z + 4 - oz) % 4) * 4 + (x + 4 - ox) % 4


def slot_group(c):
    return (c * 2731) >> 16


LOG2E = 1.4426950408889634
PARTS = (((2, 0, 1), 48, 0), ((0, 1, 2), 40, 48), ((1, 2, 0), 40, 88))
QCOLS = 512
KEYS = 1024
UNITS_KV = 8
VROWS = 144


def group_shift(k):
    return k + k // 2 - 2 * (k // 3)


def layer_kernel(
    x_ref, mod_ref, ids_ref, rw_ref, wgu_hbm, wd_hbm, gain_ref, wq_hbm, wkv_hbm, qg_ref, kg_ref,
    ho_ref, att_ref,
    kvw_s, out_s, a_s, b_s, ret_s, rin_s, ps_s, pr_s, val_s, hi_s, lo_s, valt_s, acc_s, nrm_s, q_s,
    buf0, buf1, buf2,
    wsem, dsend, drecv, fsend, frecv, psend, precv, rsend, rrecv, hsend, hrecv, ssem, rsem,
):
    me = lax.axis_index("expert")
    core = lax.axis_index("half")
    mate = 1 - core
    own = pl.multiple_of(core * HD, HD)
    oth = pl.multiple_of(mate * HD, HD)
    place = (me // 16, (me // 4) % 4, me % 4)
    bufs = (buf0, buf1, buf2)

    barrier = pltpu.get_barrier_semaphore()
    pl.semaphore_signal(barrier, inc=1, device_id={"expert": me, "half": mate}, device_id_type=MESH)

    @pl.loop(1, CHIPS)
    def _(n):
        pl.semaphore_signal(
            barrier, inc=1, device_id={"expert": chip_plus(me, n), "half": core}, device_id_type=MESH
        )

    row = lax.broadcasted_iota(jnp.int32, (TOK, TOK), 0)
    lane = lax.broadcasted_iota(jnp.int32, (TOK, TOK), 1)
    ra, rb, rc = row >> 4, (row >> 2) & 3, row & 3
    my_y, my_z, my_x = me // 16, (me // 4) % 4, me % 4
    target = ((my_y + rc) & 3) * 16 + ((my_z + rc + rb) & 3) * 4 + ((my_x + rc + ra) & 3)
    target = jnp.where(row < CHIPS, target, -1)
    member = jnp.zeros((TOK, TOK), F32)
    weight = jnp.zeros((TOK, TOK), F32)
    for j in range(ids_ref.shape[0]):
        hit = jnp.broadcast_to(ids_ref[j : j + 1, :], (TOK, TOK)) == target
        member = member + jnp.where(hit, 1.0, 0.0)
        weight = weight + jnp.where(hit, jnp.broadcast_to(rw_ref[j : j + 1, :], (TOK, TOK)), 0.0)
    earlier = jnp.where(row < lane, 1.0, 0.0).astype(BF16)
    rank = jnp.dot(member.astype(BF16), earlier, preferred_element_type=F32)
    val = jnp.where(member > 0.5, rank, -1.0)
    valt_s[...] = val.astype(BF16)
    val_s[...] = val.T.astype(BF16)
    weight = weight.T
    high = weight.astype(BF16)
    hi_s[...] = high
    lo_s[...] = (weight - high.astype(F32)).astype(BF16)

    pl.semaphore_wait(barrier, CHIPS)

    def pieces(ref, b):
        return ref.at[pl.ds(b * PER, PER)]

    def experts(wraw, w_s, wd_s, kvraw, gu_s, own_s, mask_s):
        loads = [
            pltpu.make_async_copy(wgu_hbm, wraw, wsem.at[0]),
            pltpu.make_async_copy(wd_hbm, wd_s, wsem.at[1]),
            pltpu.make_async_copy(wkv_hbm, kvraw, wsem.at[2]),
        ]
        for load in loads:
            load.start()

        def dispatch(b):
            @pl.loop(0, PER)
            def _(i):
                n = b * PER + i

                @pl.when(n == 0)
                def _():
                    pltpu.make_async_copy(out_s.at[0], a_s.at[0], drecv.at[0]).start()

                @pl.when(n > 0)
                def _():
                    pltpu.make_async_remote_copy(
                        src_ref=out_s.at[n],
                        dst_ref=a_s.at[n],
                        send_sem=dsend,
                        recv_sem=drecv.at[b],
                        device_id={"expert": chip_plus(me, n), "half": core},
                        device_id_type=MESH,
                    ).start()

        x_own = x_ref[:, pl.ds(own, HD)]

        @pl.loop(0, BATCHES)
        def _(b):
            c = lax.broadcasted_iota(jnp.int32, (ROWS, TOK), 0) + b * ROWS
            group = slot_group(c)
            spread = jnp.where(group == lax.broadcasted_iota(jnp.int32, (ROWS, TOK), 1), 1.0, 0.0)
            vals = jnp.dot(spread.astype(BF16), valt_s[...], preferred_element_type=F32)
            pick = jnp.where(vals == (c - CAP * group).astype(F32), 1.0, 0.0).astype(BF16)
            rows_out = jnp.dot(pick, x_own, preferred_element_type=F32).astype(BF16)
            out_s[pl.ds(b * PER, PER)] = rows_out.reshape(PER, CAP, HD)

            @pl.when(b < AHEAD)
            def _():
                dispatch(b)

        @pl.loop(0, CHIPS)
        def _(n):
            mask_s[n] = jnp.full((CAP, 128), mod_ref[chip_minus(me, n), 0], jnp.int32).astype(F32)

        prow = lax.broadcasted_iota(jnp.int32, (256, 256), 0)
        pcol = lax.broadcasted_iota(jnp.int32, (256, 256), 1)
        part = jnp.where(pcol == jnp.where(prow < 128, 2 * prow, 2 * prow - 255), 1.0, 0.0).astype(BF16)
        loads[0].wait()

        @pl.loop(0, D // 128)
        def _(r):
            r0 = pl.multiple_of(r * 128, 128)
            for e in range(2):
                block = wraw[e, pl.ds(r0, 128)].reshape(256, UNITS)
                parted = jnp.dot(part, block, preferred_element_type=F32).astype(BF16)
                w_s[pl.ds(r0, 128), e * 2 * UNITS : e * 2 * UNITS + UNITS] = parted[:128]
                w_s[pl.ds(r0, 128), e * 2 * UNITS + UNITS : (e + 1) * 2 * UNITS] = parted[128:]

        loads[2].wait()

        @pl.loop(0, D // 128)
        def _(r):
            r0 = pl.multiple_of(r * 128, 128)
            block = kvraw[pl.ds(r0, 128)].reshape(256, 256)
            parted = jnp.dot(part, block, preferred_element_type=F32).astype(BF16)
            kvw_s[pl.ds(r0, 128), 0:256] = parted[:128]
            kvw_s[pl.ds(r0, 128), 256:512] = parted[128:]

        loads[1].wait()

        def forward(b):
            pltpu.make_async_copy(pieces(a_s, b), pieces(a_s, b), drecv.at[b]).wait()
            pltpu.make_async_remote_copy(
                src_ref=pieces(a_s, b),
                dst_ref=pieces(b_s, b),
                send_sem=fsend.at[b],
                recv_sem=frecv.at[b],
                device_id={"expert": me, "half": mate},
                device_id_type=MESH,
            ).start()

        forward(0)

        @pl.loop(0, BATCHES)
        def _(b):
            pltpu.make_async_remote_copy(
                src_ref=pieces(a_s, b),
                dst_ref=pieces(b_s, b),
                send_sem=fsend.at[b],
                recv_sem=frecv.at[b],
                device_id={"expert": me, "half": mate},
                device_id_type=MESH,
            ).wait()
            xa = a_s[pl.ds(b * PER, PER)].reshape(ROWS, HD)
            xb = b_s[pl.ds(b * PER, PER)].reshape(ROWS, HD)

            @pl.loop(0, 4)
            def _(k):
                cols = pl.ds(pl.multiple_of(k * UNITS, 128), UNITS)
                gu_s[:, cols] = jnp.dot(
                    xa, w_s[pl.ds(own, HD), cols], preferred_element_type=F32
                ) + jnp.dot(xb, w_s[pl.ds(oth, HD), cols], preferred_element_type=F32)

            mask = mask_s[pl.ds(b * PER, PER)].reshape(ROWS, 128)
            image = jnp.concatenate([mask, mask, mask], axis=1) > 0.5
            gate = jnp.where(image, gu_s[:, 2 * UNITS : 3 * UNITS], gu_s[:, :UNITS])
            up = jnp.where(image, gu_s[:, 3 * UNITS :], gu_s[:, UNITS : 2 * UNITS])
            act = gate / (1.0 + jnp.exp(-gate)) * up
            both = jnp.concatenate(
                [jnp.where(image, 0.0, act), jnp.where(image, act, 0.0)], axis=1
            ).astype(BF16)

            ps_s[...] = jnp.dot(both, wd_s[:, pl.ds(oth, HD)], preferred_element_type=F32)
            swap = pltpu.make_async_remote_copy(
                src_ref=ps_s,
                dst_ref=pr_s.at[b % 2],
                send_sem=psend,
                recv_sem=precv.at[b % 2],
                device_id={"expert": me, "half": mate},
                device_id_type=MESH,
            )
            swap.start()
            own_s[...] = jnp.dot(both, wd_s[:, pl.ds(own, HD)], preferred_element_type=F32)
            swap.wait()
            ret_s[pl.ds(b * PER, PER)] = (own_s[...] + pr_s[b % 2]).astype(BF16).reshape(PER, CAP, HD)

            @pl.loop(0, PER)
            def _(i):
                n = b * PER + i

                @pl.when(n == 0)
                def _():
                    pltpu.make_async_copy(ret_s.at[0], rin_s.at[0], rrecv.at[0]).start()

                @pl.when(n > 0)
                def _():
                    pltpu.make_async_remote_copy(
                        src_ref=ret_s.at[n],
                        dst_ref=rin_s.at[n],
                        send_sem=rsend,
                        recv_sem=rrecv.at[b],
                        device_id={"expert": chip_minus(me, n), "half": core},
                        device_id_type=MESH,
                    ).start()

            @pl.when(b + AHEAD < BATCHES)
            def _():
                dispatch(b + AHEAD)

            @pl.when(b < BATCHES - 1)
            def _():
                forward(b + 1)


    pl.run_scoped(
        experts,
        pltpu.VMEM((2, D, 2, UNITS), BF16),
        pltpu.VMEM((D, 4 * UNITS), BF16),
        pltpu.VMEM((2 * UNITS, D), BF16),
        pltpu.VMEM((D, 2, 256), BF16),
        pltpu.VMEM((ROWS, 4 * UNITS), F32),
        pltpu.VMEM((ROWS, HD), F32),
        pltpu.VMEM((CHIPS, CAP, 128), F32),
    )

    def along(i, axis):
        return 1 - ((i + 6 - axis - core) % 3 + 1) // 2

    def coordinate(axis):
        return sum(place[i] * along(i, axis) for i in range(3))

    def neighbour(axis, step):
        moved = [(place[i] + step * along(i, axis)) % 4 for i in range(3)]
        return {"expert": moved[0] * 16 + moved[1] * 4 + moved[2], "half": core}

    def send(p, view, phase, step, mark):
        pltpu.make_async_remote_copy(
            src_ref=view,
            dst_ref=view,
            send_sem=ssem.at[p, phase],
            recv_sem=rsem.at[p, mark],
            device_id=neighbour(PARTS[p][0][phase], step),
            device_id_type=MESH,
        ).start()

    def landed(p, view, mark):
        pltpu.make_async_copy(view, view, rsem.at[p, mark]).wait()

    early, late, every = pl.ds(0, 2), pl.ds(2, 2), pl.ds(0, 4)

    def one(p, shift, kinds):
        a, b, c = spots[p]
        return bufs[p].at[c, kinds, b, (a + shift) % 4]

    def line(p, shift, kinds):
        a, b, c = spots[p]
        return bufs[p].at[c, kinds, (b + shift) % 4]

    def sheet(p, shift, k, kinds):
        a, b, c = spots[p]
        return bufs[p].at[(c + shift) % 4, kinds, (b + group_shift(k)) % 4]

    def ring(view, phase, base):
        for p in range(3):
            send(p, view(p, 0, every), phase, 1, base)
            send(p, view(p, 0, every), phase, 3, base + 1)

    def pass_on(view, phase, base):
        for p in range(3):
            landed(p, view(p, 3, every), base)
            landed(p, view(p, 1, every), base + 1)
            send(p, view(p, 3, early), phase, 1, base + 2)
            send(p, view(p, 1, late), phase, 3, base + 3)

    def opposite(view, base):
        for p in range(3):
            landed(p, view(p, 2, early), base + 2)
            landed(p, view(p, 2, late), base + 3)

    def group(k):
        return lambda p, shift, kinds: sheet(p, shift, k, kinds)

    spots = [tuple(coordinate(axis) for axis in axes) for axes, _, _ in PARTS]

    def head_norm(values, gain):
        scale = lax.rsqrt(jnp.mean(values * values, axis=-1, keepdims=True) + EPSILON)
        return (values * scale * gain).astype(BF16)

    def project(wq_s):
        load = pltpu.make_async_copy(wq_hbm, wq_s, wsem.at[0])
        load.start()
        acc_s[...] = x_ref[:, pl.ds(own, HD)].astype(F32)
        wide = 2 * ROWS

        @pl.loop(0, BATCHES // 2)
        def _(b):
            c = lax.broadcasted_iota(jnp.int32, (TOK, wide), 1) + b * wide
            group = slot_group(c)
            spread = jnp.where(group == lax.broadcasted_iota(jnp.int32, (TOK, wide), 0), 1.0, 0.0).astype(BF16)
            vals = jnp.dot(val_s[...], spread, preferred_element_type=F32)
            pick = vals == (c - CAP * group).astype(F32)
            w_hi = jnp.where(pick, jnp.dot(hi_s[...], spread, preferred_element_type=F32), 0.0).astype(BF16)
            w_lo = jnp.where(pick, jnp.dot(lo_s[...], spread, preferred_element_type=F32), 0.0).astype(BF16)
            for k in range(2):
                pltpu.make_async_copy(pieces(rin_s, 2 * b + k), pieces(rin_s, 2 * b + k), rrecv.at[2 * b + k]).wait()
            back = rin_s[pl.ds(b * 2 * PER, 2 * PER)].reshape(wide, HD)
            acc_s[...] += jnp.dot(w_hi, back, preferred_element_type=F32) + jnp.dot(
                w_lo, back, preferred_element_type=F32
            )

        ho_ref[:, pl.ds(own, HD)] = acc_s[...]
        share = pltpu.make_async_remote_copy(
            src_ref=acc_s,
            dst_ref=ho_ref.at[:, pl.ds(own, HD)],
            send_sem=hsend,
            recv_sem=hrecv,
            device_id={"expert": me, "half": mate},
            device_id_type=MESH,
        )
        share.start()
        share.wait()
        hidden = ho_ref[...]
        mean_sq = jnp.mean(hidden * hidden, axis=-1, keepdims=True)
        nrm_s[...] = (hidden * lax.rsqrt(mean_sq + EPSILON) * gain_ref[...]).astype(BF16)


        for group_of in range(2):
            pair = jnp.dot(
                nrm_s[...], kvw_s[:, group_of * 256 : (group_of + 1) * 256], preferred_element_type=F32
            )
            for i in range(2):
                rows_kv = pair[:, i * 128 : (i + 1) * 128]
                rows_kv = head_norm(rows_kv, kg_ref[...]) if group_of == 0 else rows_kv.astype(BF16)
                for p, (_, rows, first) in enumerate(PARTS):
                    a, b, c = spots[p]
                    bufs[p][c, 2 * group_of + i, b, a] = rows_kv[first : first + rows]
        ring(one, 0, 0)
        load.wait()

        def queries(first, last):
            @pl.loop(first, last)
            def _(k):
                cols = pl.ds(pl.multiple_of(k * 256, 256), 256)
                q2 = jnp.dot(nrm_s[...], wq_s[:, cols], preferred_element_type=F32)
                for i in range(2):
                    rows_q = pl.ds(pl.multiple_of((2 * (k % 4) + i) * 128, 128), 128)
                    q_s[k // 4, rows_q] = head_norm(q2[:, i * 128 : (i + 1) * 128], qg_ref[...])

        queries(0, 3)
        pass_on(one, 0, 0)
        queries(3, 5)
        opposite(one, 0)
        ring(line, 1, 4)
        ring(group(0), 2, 8)
        queries(5, 8)

    pl.run_scoped(project, pltpu.VMEM((D, D), BF16))

    pass_on(line, 1, 4)
    ring(group(1), 2, 12)
    ring(group(2), 2, 16)

    def attend(kun, vun, vt_s, s0, s1, m_s, sum_s):
        m_s[...] = jnp.full_like(m_s, -1e30)
        sum_s[...] = jnp.zeros_like(sum_s)
        vt_s[:, 128:, :] = jnp.ones((2, VROWS - 128, KEYS), BF16)
        scale = 128**-0.5 * LOG2E

        def scores(h, r):
            cols = pl.ds(pl.multiple_of(r * QCOLS, QCOLS), QCOLS)
            return lax.dot_general(kun[h], q_s[h, cols], (((1,), (1,)), ((), ())), preferred_element_type=F32)

        def absorb(h, s_ref, r):
            cols = pl.ds(pl.multiple_of(r * QCOLS, QCOLS), QCOLS)
            s = s_ref[...]
            m_old = m_s[h, :, cols]
            m_new = jnp.maximum(m_old, jnp.max(s, axis=0, keepdims=True))
            m_s[h, :, cols] = m_new
            probs = jnp.exp2(s * scale - m_new * scale).astype(BF16)
            fade = jnp.exp2((m_old - m_new) * scale)
            sum_s[h, :, cols] = sum_s[h, :, cols] * fade + jnp.dot(vt_s[h], probs, preferred_element_type=F32)

        steps = q_s.shape[1] // QCOLS

        @pl.loop(0, UNITS_KV)
        def _(u):
            @pl.when(u == 1)
            def _():
                opposite(line, 4)
                ring(group(3), 2, 20)

            for k in range(4):

                @pl.when(u == 2 + k)
                def _(k=k):
                    pass_on(group(k), 2, 8 + 4 * k)

            for k in range(2):

                @pl.when(u == 6 + k)
                def _(k=k):
                    opposite(group(2 * k), 8 + 8 * k)
                    opposite(group(2 * k + 1), 12 + 8 * k)

            stage = u // 2
            mid = (stage % 3 + 1) // 2
            start = 0
            for p, (axes, rows, first) in enumerate(PARTS):
                a, b, c = spots[p]
                for i in range(2):
                    shift_c = (1 - mid) * 2 * (stage // 3) + mid * (3 - 2 * i)
                    k = (1 - mid) * (2 * (u % 2) + i) + mid * (u - 2)
                    at_c, at_b = (c + shift_c) % 4, (b + group_shift(k)) % 4
                    for h in range(2):
                        kun[h, start : start + 4 * rows] = bufs[p][at_c, h, at_b].reshape(4 * rows, 128)
                        vun[h, start : start + 4 * rows] = bufs[p][at_c, 2 + h, at_b].reshape(4 * rows, 128)
                    start += 4 * rows
            for h in range(2):
                vt_s[h, :128, :] = vun[h].T

            s0[...] = scores(0, 0)

            @pl.loop(0, steps)
            def _(r):
                s1[...] = scores(1, r)
                absorb(0, s0, r)
                s0[...] = scores(0, lax.rem(r + 1, steps))
                absorb(1, s1, r)

        for h in range(2):
            for j in range(8):
                cols = slice(j * 128, (j + 1) * 128)
                head = sum_s[h, :128, cols] / sum_s[h, 128:129, cols]
                att_ref[:, (h * 8 + j) * 128 : (h * 8 + j + 1) * 128] = head.T.astype(BF16)


    pl.run_scoped(
        attend,
        pltpu.VMEM((2, KEYS, 128), BF16),
        pltpu.VMEM((2, KEYS, 128), BF16),
        pltpu.VMEM((2, VROWS, KEYS), BF16),
        pltpu.VMEM((KEYS, QCOLS), F32),
        pltpu.VMEM((KEYS, QCOLS), F32),
        pltpu.VMEM((2, 1, 1024), F32),
        pltpu.VMEM((2, VROWS, 1024), F32),
    )

    three = pl.ds(0, 3)
    for p in range(3):
        a, b, c = spots[p]
        view = bufs[p].at[c, :, b, three]
        pltpu.make_async_copy(view, view, ssem.at[p, 0]).wait()
        view = bufs[p].at[c, :, three]
        pltpu.make_async_copy(view, view, ssem.at[p, 1]).wait()
        view = bufs[p].at[three]
        pltpu.make_async_copy(view, view, ssem.at[p, 2]).wait()
    rest = pl.ds(1, CHIPS - 1)
    pltpu.make_async_copy(out_s.at[rest], out_s.at[rest], dsend).wait()
    pltpu.make_async_copy(ret_s.at[rest], ret_s.at[rest], rsend).wait()


def layer_call(x, mod, ids, rw, wgu, wd, gain, wq, wkv, qg, kg):
    vm = pl.BlockSpec(memory_space=pltpu.VMEM)
    hbm = pl.BlockSpec(memory_space=pl.ANY)
    sm = pl.BlockSpec(memory_space=pltpu.SMEM)
    dma = pltpu.SemaphoreType.DMA
    return pl.pallas_call(
        layer_kernel,
        out_shape=(jax.ShapeDtypeStruct((TOK, D), F32), jax.ShapeDtypeStruct((TOK, D), BF16)),
        in_specs=[vm, sm, vm, vm, hbm, hbm, vm, hbm, hbm, vm, vm],
        out_specs=(vm, vm),
        scratch_shapes=[
            pltpu.VMEM((D, 512), BF16),
            pltpu.VMEM((CHIPS, CAP, HD), BF16),
            pltpu.VMEM((CHIPS, CAP, HD), BF16),
            pltpu.VMEM((CHIPS, CAP, HD), BF16),
            pltpu.VMEM((CHIPS, CAP, HD), BF16),
            pltpu.VMEM((CHIPS, CAP, HD), BF16),
            pltpu.VMEM((ROWS, HD), F32),
            pltpu.VMEM((2, ROWS, HD), F32),
            pltpu.VMEM((TOK, TOK), BF16),
            pltpu.VMEM((TOK, TOK), BF16),
            pltpu.VMEM((TOK, TOK), BF16),
            pltpu.VMEM((TOK, TOK), BF16),
            pltpu.VMEM((TOK, HD), F32),
            pltpu.VMEM((TOK, D), BF16),
            pltpu.VMEM((2, 8 * TOK, 128), BF16),
        ]
        + [pltpu.VMEM((4, 4, 4, 4, rows, 128), BF16) for _, rows, _ in PARTS]
        + [
            dma((3,)),
            dma,
            dma((BATCHES,)),
            dma((BATCHES,)),
            dma((BATCHES,)),
            dma,
            dma((2,)),
            dma,
            dma((BATCHES,)),
            dma,
            dma,
            dma((3, 3)),
            dma((3, 24)),
        ],
        compiler_params=pltpu.CompilerParams(
            collective_id=0, has_side_effects=True, vmem_limit_bytes=62 * 1024 * 1024
        ),
    )(x, mod, ids, rw, wgu, wd, gain, wq, wkv, qg, kg)


def body(hidden_in, modality, expert_ids, route_weights, w_gate_up, w_down, norm_gain, w_query,
         key_value_weight, q_gain, k_gain):
    return layer_call(
        hidden_in, modality.reshape(CHIPS, TOK), expert_ids.T, route_weights.T, w_gate_up,
        w_down.reshape(2 * UNITS, D), norm_gain.reshape(1, D), w_query, key_value_weight,
        q_gain.reshape(1, 128), k_gain.reshape(1, 128),
    )


def solution(mesh):
    in_specs = (
        P("expert", None), P(), P("expert", None), P("expert", None),
        P("expert", None, None, "half"), P("expert", "half", None), P(), P(None, "half"),
        P(None, None, "half"), P(), P(),
    )
    out_specs = (P("expert", None), P("expert", "half"))
    return jax.shard_map(body, mesh=mesh, in_specs=in_specs, out_specs=out_specs, check_vma=False)
```

```python
import functools
import jax
import jax.numpy as jnp
from jax import lax
from jax.experimental import pallas as pl
from jax.experimental.pallas import tpu as pltpu
from jax.sharding import PartitionSpec as P

EPSILON = 1e-06
MESH = pl.DeviceIdType.MESH
F32 = jnp.float32
BF16 = jnp.bfloat16

CHIPS = 64
CAP = 24
TOK = 128
D = 2048
HD = 1024
UNITS = 384
PER = 8
BATCHES = CHIPS // PER
ROWS = PER * CAP
AHEAD = 4


def offsets(n):
    a, b, c = n // 16, (n // 4) % 4, n % 4
    return c, (c + b) % 4, (c + a) % 4


def chip_plus(chip, n):
    oy, oz, ox = offsets(n)
    y, z, x = chip // 16, (chip // 4) % 4, chip % 4
    return ((y + oy) % 4) * 16 + ((z + oz) % 4) * 4 + (x + ox) % 4


def chip_minus(chip, n):
    oy, oz, ox = offsets(n)
    y, z, x = chip // 16, (chip // 4) % 4, chip % 4
    return ((y + 4 - oy) % 4) * 16 + ((z + 4 - oz) % 4) * 4 + (x + 4 - ox) % 4


def slot_group(c):
    return (c * 2731) >> 16


LOG2E = 1.4426950408889634
PARTS = (((2, 0, 1), 48, 0), ((0, 1, 2), 40, 48), ((1, 2, 0), 40, 88))
QCOLS = 512
KEYS = 1024
UNITS_KV = 8
VROWS = 144


def group_shift(k):
    return k + k // 2 - 2 * (k // 3)


def layer_kernel(
    x_ref, mod_ref, ids_ref, rw_ref, wgu_hbm, wd_hbm, gain_ref, wq_hbm, wkv_hbm, qg_ref, kg_ref,
    ho_ref, att_ref,
    kvw_s, out_s, a_s, b_s, ret_s, rin_s, ps_s, pr_s, val_s, hi_s, lo_s, valt_s, acc_s, nrm_s, q_s,
    buf0, buf1, buf2,
    wsem, dsend, drecv, fsend, frecv, psend, precv, rsend, rrecv, hsend, hrecv, ssem, rsem,
):
    me = lax.axis_index("expert")
    core = lax.axis_index("half")
    mate = 1 - core
    own = pl.multiple_of(core * HD, HD)
    oth = pl.multiple_of(mate * HD, HD)
    place = (me // 16, (me // 4) % 4, me % 4)
    bufs = (buf0, buf1, buf2)

    barrier = pltpu.get_barrier_semaphore()
    pl.semaphore_signal(barrier, inc=1, device_id={"expert": me, "half": mate}, device_id_type=MESH)

    @pl.loop(1, CHIPS)
    def _(n):
        pl.semaphore_signal(
            barrier, inc=1, device_id={"expert": chip_plus(me, n), "half": core}, device_id_type=MESH
        )

    row = lax.broadcasted_iota(jnp.int32, (TOK, TOK), 0)
    lane = lax.broadcasted_iota(jnp.int32, (TOK, TOK), 1)
    ra, rb, rc = row >> 4, (row >> 2) & 3, row & 3
    my_y, my_z, my_x = me // 16, (me // 4) % 4, me % 4
    target = ((my_y + rc) & 3) * 16 + ((my_z + rc + rb) & 3) * 4 + ((my_x + rc + ra) & 3)
    target = jnp.where(row < CHIPS, target, -1)
    member = jnp.zeros((TOK, TOK), F32)
    weight = jnp.zeros((TOK, TOK), F32)
    for j in range(ids_ref.shape[0]):
        hit = jnp.broadcast_to(ids_ref[j : j + 1, :], (TOK, TOK)) == target
        member = member + jnp.where(hit, 1.0, 0.0)
        weight = weight + jnp.where(hit, jnp.broadcast_to(rw_ref[j : j + 1, :], (TOK, TOK)), 0.0)
    earlier = jnp.where(row < lane, 1.0, 0.0).astype(BF16)
    rank = jnp.dot(member.astype(BF16), earlier, preferred_element_type=F32)
    val = jnp.where(member > 0.5, rank, -1.0)
    valt_s[...] = val.astype(BF16)
    val_s[...] = val.T.astype(BF16)
    weight = weight.T
    high = weight.astype(BF16)
    hi_s[...] = high
    lo_s[...] = (weight - high.astype(F32)).astype(BF16)

    pl.semaphore_wait(barrier, CHIPS)

    def pieces(ref, b):
        return ref.at[pl.ds(b * PER, PER)]

    def experts(wraw, w_s, wd_s, kvraw, gu_s, own_s, mask_s):
        loads = [
            pltpu.make_async_copy(wgu_hbm, wraw, wsem.at[0]),
            pltpu.make_async_copy(wd_hbm, wd_s, wsem.at[1]),
            pltpu.make_async_copy(wkv_hbm, kvraw, wsem.at[2]),
        ]
        for load in loads:
            load.start()

        def dispatch(b):
            @pl.loop(0, PER)
            def _(i):
                n = b * PER + i

                @pl.when(n == 0)
                def _():
                    pltpu.make_async_copy(out_s.at[0], a_s.at[0], drecv.at[0]).start()

                @pl.when(n > 0)
                def _():
                    pltpu.make_async_remote_copy(
                        src_ref=out_s.at[n],
                        dst_ref=a_s.at[n],
                        send_sem=dsend,
                        recv_sem=drecv.at[b],
                        device_id={"expert": chip_plus(me, n), "half": core},
                        device_id_type=MESH,
                    ).start()

        x_own = x_ref[:, pl.ds(own, HD)]

        @pl.loop(0, BATCHES)
        def _(b):
            c = lax.broadcasted_iota(jnp.int32, (ROWS, TOK), 0) + b * ROWS
            group = slot_group(c)
            spread = jnp.where(group == lax.broadcasted_iota(jnp.int32, (ROWS, TOK), 1), 1.0, 0.0)
            vals = jnp.dot(spread.astype(BF16), valt_s[...], preferred_element_type=F32)
            pick = jnp.where(vals == (c - CAP * group).astype(F32), 1.0, 0.0).astype(BF16)
            rows_out = jnp.dot(pick, x_own, preferred_element_type=F32).astype(BF16)
            out_s[pl.ds(b * PER, PER)] = rows_out.reshape(PER, CAP, HD)

            @pl.when(b < AHEAD)
            def _():
                dispatch(b)

        @pl.loop(0, CHIPS)
        def _(n):
            mask_s[n] = jnp.full((CAP, 128), mod_ref[chip_minus(me, n), 0], jnp.int32).astype(F32)

        prow = lax.broadcasted_iota(jnp.int32, (256, 256), 0)
        pcol = lax.broadcasted_iota(jnp.int32, (256, 256), 1)
        part = jnp.where(pcol == jnp.where(prow < 128, 2 * prow, 2 * prow - 255), 1.0, 0.0).astype(BF16)
        loads[0].wait()

        @pl.loop(0, D // 128)
        def _(r):
            r0 = pl.multiple_of(r * 128, 128)
            for e in range(2):
                block = wraw[e, pl.ds(r0, 128)].reshape(256, UNITS)
                parted = jnp.dot(part, block, preferred_element_type=F32).astype(BF16)
                w_s[pl.ds(r0, 128), e * 2 * UNITS : e * 2 * UNITS + UNITS] = parted[:128]
                w_s[pl.ds(r0, 128), e * 2 * UNITS + UNITS : (e + 1) * 2 * UNITS] = parted[128:]

        loads[2].wait()

        @pl.loop(0, D // 128)
        def _(r):
            r0 = pl.multiple_of(r * 128, 128)
            block = kvraw[pl.ds(r0, 128)].reshape(256, 256)
            parted = jnp.dot(part, block, preferred_element_type=F32).astype(BF16)
            kvw_s[pl.ds(r0, 128), 0:256] = parted[:128]
            kvw_s[pl.ds(r0, 128), 256:512] = parted[128:]

        loads[1].wait()

        def forward(b):
            pltpu.make_async_copy(pieces(a_s, b), pieces(a_s, b), drecv.at[b]).wait()
            pltpu.make_async_remote_copy(
                src_ref=pieces(a_s, b),
                dst_ref=pieces(b_s, b),
                send_sem=fsend.at[b],
                recv_sem=frecv.at[b],
                device_id={"expert": me, "half": mate},
                device_id_type=MESH,
            ).start()

        def swap(b):
            return pltpu.make_async_remote_copy(
                src_ref=ps_s.at[b % 2],
                dst_ref=pr_s.at[b % 3],
                send_sem=psend.at[b % 2],
                recv_sem=precv.at[b % 3],
                device_id={"expert": me, "half": mate},
                device_id_type=MESH,
            )

        forward(0)

        @pl.loop(0, BATCHES + 1)
        def _(b):
            @pl.when(b < BATCHES - 1)
            def _():
                forward(b + 1)

            @pl.when(b < BATCHES)
            def _():
                pltpu.make_async_remote_copy(
                    src_ref=pieces(a_s, b),
                    dst_ref=pieces(b_s, b),
                    send_sem=fsend.at[b],
                    recv_sem=frecv.at[b],
                    device_id={"expert": me, "half": mate},
                    device_id_type=MESH,
                ).wait()
                xa = a_s[pl.ds(b * PER, PER)].reshape(ROWS, HD)
                xb = b_s[pl.ds(b * PER, PER)].reshape(ROWS, HD)

                @pl.loop(0, 4)
                def _(k):
                    cols = pl.ds(pl.multiple_of(k * UNITS, 128), UNITS)
                    gu_s[:, cols] = jnp.dot(
                        xa, w_s[pl.ds(own, HD), cols], preferred_element_type=F32
                    ) + jnp.dot(xb, w_s[pl.ds(oth, HD), cols], preferred_element_type=F32)

                mask = mask_s[pl.ds(b * PER, PER)].reshape(ROWS, 128)
                image = jnp.concatenate([mask, mask, mask], axis=1) > 0.5
                gate = jnp.where(image, gu_s[:, 2 * UNITS : 3 * UNITS], gu_s[:, :UNITS])
                up = jnp.where(image, gu_s[:, 3 * UNITS :], gu_s[:, UNITS : 2 * UNITS])
                act = gate / (1.0 + jnp.exp(-gate)) * up
                both = jnp.concatenate(
                    [jnp.where(image, 0.0, act), jnp.where(image, act, 0.0)], axis=1
                ).astype(BF16)
                ps_s[b % 2] = jnp.dot(both, wd_s[:, pl.ds(oth, HD)], preferred_element_type=F32)
                swap(b).start()
                own_s[b % 2] = jnp.dot(both, wd_s[:, pl.ds(own, HD)], preferred_element_type=F32)

            @pl.when(b > 0)
            def _():
                done = b - 1
                swap(done).wait()
                ret_s[pl.ds(done * PER, PER)] = (
                    (own_s[done % 2] + pr_s[done % 3]).astype(BF16).reshape(PER, CAP, HD)
                )

                @pl.loop(0, PER)
                def _(i):
                    n = done * PER + i

                    @pl.when(n == 0)
                    def _():
                        pltpu.make_async_copy(ret_s.at[0], rin_s.at[0], rrecv.at[0]).start()

                    @pl.when(n > 0)
                    def _():
                        pltpu.make_async_remote_copy(
                            src_ref=ret_s.at[n],
                            dst_ref=rin_s.at[n],
                            send_sem=rsend,
                            recv_sem=rrecv.at[done],
                            device_id={"expert": chip_minus(me, n), "half": core},
                            device_id_type=MESH,
                        ).start()

            @pl.when(b + AHEAD < BATCHES)
            def _():
                dispatch(b + AHEAD)

    pl.run_scoped(
        experts,
        pltpu.VMEM((2, D, 2, UNITS), BF16),
        pltpu.VMEM((D, 4 * UNITS), BF16),
        pltpu.VMEM((2 * UNITS, D), BF16),
        pltpu.VMEM((D, 2, 256), BF16),
        pltpu.VMEM((ROWS, 4 * UNITS), F32),
        pltpu.VMEM((2, ROWS, HD), F32),
        pltpu.VMEM((CHIPS, CAP, 128), F32),
    )

    def along(i, axis):
        return 1 - ((i + 6 - axis - core) % 3 + 1) // 2

    def coordinate(axis):
        return sum(place[i] * along(i, axis) for i in range(3))

    def neighbour(axis, step):
        moved = [(place[i] + step * along(i, axis)) % 4 for i in range(3)]
        return {"expert": moved[0] * 16 + moved[1] * 4 + moved[2], "half": core}

    def send(p, view, phase, step, mark):
        pltpu.make_async_remote_copy(
            src_ref=view,
            dst_ref=view,
            send_sem=ssem.at[p, phase],
            recv_sem=rsem.at[p, mark],
            device_id=neighbour(PARTS[p][0][phase], step),
            device_id_type=MESH,
        ).start()

    def landed(p, view, mark):
        pltpu.make_async_copy(view, view, rsem.at[p, mark]).wait()

    early, late, every = pl.ds(0, 2), pl.ds(2, 2), pl.ds(0, 4)

    def one(p, shift, kinds):
        a, b, c = spots[p]
        return bufs[p].at[c, kinds, b, (a + shift) % 4]

    def line(p, shift, kinds):
        a, b, c = spots[p]
        return bufs[p].at[c, kinds, (b + shift) % 4]

    def sheet(p, shift, k, kinds):
        a, b, c = spots[p]
        return bufs[p].at[(c + shift) % 4, kinds, (b + group_shift(k)) % 4]

    def ring(view, phase, base):
        for p in range(3):
            send(p, view(p, 0, every), phase, 1, base)
            send(p, view(p, 0, every), phase, 3, base + 1)

    def pass_on(view, phase, base):
        for p in range(3):
            landed(p, view(p, 3, every), base)
            landed(p, view(p, 1, every), base + 1)
            send(p, view(p, 3, early), phase, 1, base + 2)
            send(p, view(p, 1, late), phase, 3, base + 3)

    def opposite(view, base):
        for p in range(3):
            landed(p, view(p, 2, early), base + 2)
            landed(p, view(p, 2, late), base + 3)

    def group(k):
        return lambda p, shift, kinds: sheet(p, shift, k, kinds)

    spots = [tuple(coordinate(axis) for axis in axes) for axes, _, _ in PARTS]

    def head_norm(values, gain):
        scale = lax.rsqrt(jnp.mean(values * values, axis=-1, keepdims=True) + EPSILON)
        return (values * scale * gain).astype(BF16)

    def project(wq_s):
        load = pltpu.make_async_copy(wq_hbm, wq_s, wsem.at[0])
        load.start()
        acc_s[...] = x_ref[:, pl.ds(own, HD)].astype(F32)
        wide = 2 * ROWS

        @pl.loop(0, BATCHES // 2)
        def _(b):
            c = lax.broadcasted_iota(jnp.int32, (TOK, wide), 1) + b * wide
            group = slot_group(c)
            spread = jnp.where(group == lax.broadcasted_iota(jnp.int32, (TOK, wide), 0), 1.0, 0.0).astype(BF16)
            vals = jnp.dot(val_s[...], spread, preferred_element_type=F32)
            pick = vals == (c - CAP * group).astype(F32)
            w_hi = jnp.where(pick, jnp.dot(hi_s[...], spread, preferred_element_type=F32), 0.0).astype(BF16)
            w_lo = jnp.where(pick, jnp.dot(lo_s[...], spread, preferred_element_type=F32), 0.0).astype(BF16)
            for k in range(2):
                pltpu.make_async_copy(pieces(rin_s, 2 * b + k), pieces(rin_s, 2 * b + k), rrecv.at[2 * b + k]).wait()
            back = rin_s[pl.ds(b * 2 * PER, 2 * PER)].reshape(wide, HD)
            acc_s[...] += jnp.dot(w_hi, back, preferred_element_type=F32) + jnp.dot(
                w_lo, back, preferred_element_type=F32
            )

        ho_ref[:, pl.ds(own, HD)] = acc_s[...]
        share = pltpu.make_async_remote_copy(
            src_ref=acc_s,
            dst_ref=ho_ref.at[:, pl.ds(own, HD)],
            send_sem=hsend,
            recv_sem=hrecv,
            device_id={"expert": me, "half": mate},
            device_id_type=MESH,
        )
        share.start()
        share.wait()
        hidden = ho_ref[...]
        mean_sq = jnp.mean(hidden * hidden, axis=-1, keepdims=True)
        nrm_s[...] = (hidden * lax.rsqrt(mean_sq + EPSILON) * gain_ref[...]).astype(BF16)


        for group_of in range(2):
            pair = jnp.dot(
                nrm_s[...], kvw_s[:, group_of * 256 : (group_of + 1) * 256], preferred_element_type=F32
            )
            for i in range(2):
                rows_kv = pair[:, i * 128 : (i + 1) * 128]
                rows_kv = head_norm(rows_kv, kg_ref[...]) if group_of == 0 else rows_kv.astype(BF16)
                for p, (_, rows, first) in enumerate(PARTS):
                    a, b, c = spots[p]
                    bufs[p][c, 2 * group_of + i, b, a] = rows_kv[first : first + rows]
        ring(one, 0, 0)
        load.wait()

        def queries(first, last):
            @pl.loop(first, last)
            def _(k):
                cols = pl.ds(pl.multiple_of(k * 256, 256), 256)
                q2 = jnp.dot(nrm_s[...], wq_s[:, cols], preferred_element_type=F32)
                for i in range(2):
                    rows_q = pl.ds(pl.multiple_of((2 * (k % 4) + i) * 128, 128), 128)
                    q_s[k // 4, rows_q] = head_norm(q2[:, i * 128 : (i + 1) * 128], qg_ref[...])

        queries(0, 3)
        pass_on(one, 0, 0)
        queries(3, 5)
        opposite(one, 0)
        ring(line, 1, 4)
        ring(group(0), 2, 8)
        queries(5, 8)

    pl.run_scoped(project, pltpu.VMEM((D, D), BF16))

    pass_on(line, 1, 4)
    ring(group(1), 2, 12)
    ring(group(2), 2, 16)

    def attend(kun, vun, vt_s, s0, s1, m_s, sum_s):
        m_s[...] = jnp.full_like(m_s, -1e30)
        sum_s[...] = jnp.zeros_like(sum_s)
        vt_s[:, 128:, :] = jnp.ones((2, VROWS - 128, KEYS), BF16)
        scale = 128**-0.5 * LOG2E

        def scores(h, r):
            cols = pl.ds(pl.multiple_of(r * QCOLS, QCOLS), QCOLS)
            return lax.dot_general(kun[h], q_s[h, cols], (((1,), (1,)), ((), ())), preferred_element_type=F32)

        def absorb(h, s_ref, r):
            cols = pl.ds(pl.multiple_of(r * QCOLS, QCOLS), QCOLS)
            s = s_ref[...]
            m_old = m_s[h, :, cols]
            m_new = jnp.maximum(m_old, jnp.max(s, axis=0, keepdims=True))
            m_s[h, :, cols] = m_new
            probs = jnp.exp2(s * scale - m_new * scale).astype(BF16)
            fade = jnp.exp2((m_old - m_new) * scale)
            sum_s[h, :, cols] = sum_s[h, :, cols] * fade + jnp.dot(vt_s[h], probs, preferred_element_type=F32)

        steps = q_s.shape[1] // QCOLS

        @pl.loop(0, UNITS_KV)
        def _(u):
            @pl.when(u == 1)
            def _():
                opposite(line, 4)
                ring(group(3), 2, 20)

            for k in range(4):

                @pl.when(u == 2 + k)
                def _(k=k):
                    pass_on(group(k), 2, 8 + 4 * k)

            for k in range(2):

                @pl.when(u == 6 + k)
                def _(k=k):
                    opposite(group(2 * k), 8 + 8 * k)
                    opposite(group(2 * k + 1), 12 + 8 * k)

            stage = u // 2
            mid = (stage % 3 + 1) // 2
            start = 0
            for p, (axes, rows, first) in enumerate(PARTS):
                a, b, c = spots[p]
                for i in range(2):
                    shift_c = (1 - mid) * 2 * (stage // 3) + mid * (3 - 2 * i)
                    k = (1 - mid) * (2 * (u % 2) + i) + mid * (u - 2)
                    at_c, at_b = (c + shift_c) % 4, (b + group_shift(k)) % 4
                    for h in range(2):
                        kun[h, start : start + 4 * rows] = bufs[p][at_c, h, at_b].reshape(4 * rows, 128)
                        vun[h, start : start + 4 * rows] = bufs[p][at_c, 2 + h, at_b].reshape(4 * rows, 128)
                    start += 4 * rows
            for h in range(2):
                vt_s[h, :128, :] = vun[h].T

            s0[...] = scores(0, 0)

            @pl.loop(0, steps)
            def _(r):
                s1[...] = scores(1, r)
                absorb(0, s0, r)
                s0[...] = scores(0, lax.rem(r + 1, steps))
                absorb(1, s1, r)

        for h in range(2):
            for j in range(8):
                cols = slice(j * 128, (j + 1) * 128)
                head = sum_s[h, :128, cols] / sum_s[h, 128:129, cols]
                att_ref[:, (h * 8 + j) * 128 : (h * 8 + j + 1) * 128] = head.T.astype(BF16)


    pl.run_scoped(
        attend,
        pltpu.VMEM((2, KEYS, 128), BF16),
        pltpu.VMEM((2, KEYS, 128), BF16),
        pltpu.VMEM((2, VROWS, KEYS), BF16),
        pltpu.VMEM((KEYS, QCOLS), F32),
        pltpu.VMEM((KEYS, QCOLS), F32),
        pltpu.VMEM((2, 1, 1024), F32),
        pltpu.VMEM((2, VROWS, 1024), F32),
    )

    three = pl.ds(0, 3)
    for p in range(3):
        a, b, c = spots[p]
        view = bufs[p].at[c, :, b, three]
        pltpu.make_async_copy(view, view, ssem.at[p, 0]).wait()
        view = bufs[p].at[c, :, three]
        pltpu.make_async_copy(view, view, ssem.at[p, 1]).wait()
        view = bufs[p].at[three]
        pltpu.make_async_copy(view, view, ssem.at[p, 2]).wait()
    rest = pl.ds(1, CHIPS - 1)
    pltpu.make_async_copy(out_s.at[rest], out_s.at[rest], dsend).wait()
    pltpu.make_async_copy(ret_s.at[rest], ret_s.at[rest], rsend).wait()


def layer_call(x, mod, ids, rw, wgu, wd, gain, wq, wkv, qg, kg):
    vm = pl.BlockSpec(memory_space=pltpu.VMEM)
    hbm = pl.BlockSpec(memory_space=pl.ANY)
    sm = pl.BlockSpec(memory_space=pltpu.SMEM)
    dma = pltpu.SemaphoreType.DMA
    return pl.pallas_call(
        layer_kernel,
        out_shape=(jax.ShapeDtypeStruct((TOK, D), F32), jax.ShapeDtypeStruct((TOK, D), BF16)),
        in_specs=[vm, sm, vm, vm, hbm, hbm, vm, hbm, hbm, vm, vm],
        out_specs=(vm, vm),
        scratch_shapes=[
            pltpu.VMEM((D, 512), BF16),
            pltpu.VMEM((CHIPS, CAP, HD), BF16),
            pltpu.VMEM((CHIPS, CAP, HD), BF16),
            pltpu.VMEM((CHIPS, CAP, HD), BF16),
            pltpu.VMEM((CHIPS, CAP, HD), BF16),
            pltpu.VMEM((CHIPS, CAP, HD), BF16),
            pltpu.VMEM((2, ROWS, HD), F32),
            pltpu.VMEM((3, ROWS, HD), F32),
            pltpu.VMEM((TOK, TOK), BF16),
            pltpu.VMEM((TOK, TOK), BF16),
            pltpu.VMEM((TOK, TOK), BF16),
            pltpu.VMEM((TOK, TOK), BF16),
            pltpu.VMEM((TOK, HD), F32),
            pltpu.VMEM((TOK, D), BF16),
            pltpu.VMEM((2, 8 * TOK, 128), BF16),
        ]
        + [pltpu.VMEM((4, 4, 4, 4, rows, 128), BF16) for _, rows, _ in PARTS]
        + [
            dma((3,)),
            dma,
            dma((BATCHES,)),
            dma((BATCHES,)),
            dma((BATCHES,)),
            dma((2,)),
            dma((3,)),
            dma,
            dma((BATCHES,)),
            dma,
            dma,
            dma((3, 3)),
            dma((3, 24)),
        ],
        compiler_params=pltpu.CompilerParams(
            collective_id=0, has_side_effects=True, vmem_limit_bytes=62 * 1024 * 1024
        ),
    )(x, mod, ids, rw, wgu, wd, gain, wq, wkv, qg, kg)


def body(hidden_in, modality, expert_ids, route_weights, w_gate_up, w_down, norm_gain, w_query,
         key_value_weight, q_gain, k_gain):
    return layer_call(
        hidden_in, modality.reshape(CHIPS, TOK), expert_ids.T, route_weights.T, w_gate_up,
        w_down.reshape(2 * UNITS, D), norm_gain.reshape(1, D), w_query, key_value_weight,
        q_gain.reshape(1, 128), k_gain.reshape(1, 128),
    )


def solution(mesh):
    in_specs = (
        P("expert", None), P(), P("expert", None), P("expert", None),
        P("expert", None, None, "half"), P("expert", "half", None), P(), P(None, "half"),
        P(None, None, "half"), P(), P(),
    )
    out_specs = (P("expert", None), P("expert", "half"))
    return jax.shard_map(body, mesh=mesh, in_specs=in_specs, out_specs=out_specs, check_vma=False)
```

```python
import functools
import jax
import jax.numpy as jnp
from jax import lax
from jax.experimental import pallas as pl
from jax.experimental.pallas import tpu as pltpu
from jax.sharding import PartitionSpec as P

EPSILON = 1e-06
MESH = pl.DeviceIdType.MESH
F32 = jnp.float32
BF16 = jnp.bfloat16

CHIPS = 64
CAP = 24
TOK = 128
D = 2048
HD = 1024
UNITS = 384
PER = 8
BATCHES = CHIPS // PER
ROWS = PER * CAP
AHEAD = 4


def offsets(n):
    a, b, c = n // 16, (n // 4) % 4, n % 4
    return c, (c + b) % 4, (c + a) % 4


def chip_plus(chip, n):
    oy, oz, ox = offsets(n)
    y, z, x = chip // 16, (chip // 4) % 4, chip % 4
    return ((y + oy) % 4) * 16 + ((z + oz) % 4) * 4 + (x + ox) % 4


def chip_minus(chip, n):
    oy, oz, ox = offsets(n)
    y, z, x = chip // 16, (chip // 4) % 4, chip % 4
    return ((y + 4 - oy) % 4) * 16 + ((z + 4 - oz) % 4) * 4 + (x + 4 - ox) % 4


def slot_group(c):
    return (c * 2731) >> 16


LOG2E = 1.4426950408889634
PARTS = (((2, 0, 1), 48, 0), ((0, 1, 2), 40, 48), ((1, 2, 0), 40, 88))
QCOLS = 512
KEYS = 1024
UNITS_KV = 8
VROWS = 144


def group_shift(k):
    return k + k // 2 - 2 * (k // 3)


def layer_kernel(
    x_ref, mod_ref, ids_ref, rw_ref, wgu_hbm, wd_hbm, gain_ref, wq_hbm, wkv_hbm, qg_ref, kg_ref,
    ho_ref, att_ref,
    kvw_s, out_s, a_s, b_s, ret_s, rin_s, ps_s, pr_s, val_s, hi_s, lo_s, valt_s, q_s,
    buf0, buf1, buf2,
    wsem, dsend, drecv, fsend, frecv, psend, precv, rsend, rrecv, hsend, hrecv, ssem, rsem,
):
    me = lax.axis_index("expert")
    core = lax.axis_index("half")
    mate = 1 - core
    own = pl.multiple_of(core * HD, HD)
    oth = pl.multiple_of(mate * HD, HD)
    place = (me // 16, (me // 4) % 4, me % 4)
    bufs = (buf0, buf1, buf2)

    barrier = pltpu.get_barrier_semaphore()
    pl.semaphore_signal(barrier, inc=1, device_id={"expert": me, "half": mate}, device_id_type=MESH)

    @pl.loop(1, CHIPS)
    def _(n):
        pl.semaphore_signal(
            barrier, inc=1, device_id={"expert": chip_plus(me, n), "half": core}, device_id_type=MESH
        )

    row = lax.broadcasted_iota(jnp.int32, (TOK, TOK), 0)
    lane = lax.broadcasted_iota(jnp.int32, (TOK, TOK), 1)
    ra, rb, rc = row >> 4, (row >> 2) & 3, row & 3
    my_y, my_z, my_x = me // 16, (me // 4) % 4, me % 4
    target = ((my_y + rc) & 3) * 16 + ((my_z + rc + rb) & 3) * 4 + ((my_x + rc + ra) & 3)
    target = jnp.where(row < CHIPS, target, -1)
    member = jnp.zeros((TOK, TOK), F32)
    weight = jnp.zeros((TOK, TOK), F32)
    for j in range(ids_ref.shape[0]):
        hit = jnp.broadcast_to(ids_ref[j : j + 1, :], (TOK, TOK)) == target
        member = member + jnp.where(hit, 1.0, 0.0)
        weight = weight + jnp.where(hit, jnp.broadcast_to(rw_ref[j : j + 1, :], (TOK, TOK)), 0.0)
    earlier = jnp.where(row < lane, 1.0, 0.0).astype(BF16)
    rank = jnp.dot(member.astype(BF16), earlier, preferred_element_type=F32)
    val = jnp.where(member > 0.5, rank, -1.0)
    valt_s[...] = val.astype(BF16)
    val_s[...] = val.T.astype(BF16)
    weight = weight.T
    high = weight.astype(BF16)
    hi_s[...] = high
    lo_s[...] = (weight - high.astype(F32)).astype(BF16)

    pl.semaphore_wait(barrier, CHIPS)

    def pieces(ref, b):
        return ref.at[pl.ds(b * PER, PER)]

    def experts(wraw, w_s, wd_s, kvraw, gu_s, own_s, mask_s):
        loads = [
            pltpu.make_async_copy(wgu_hbm, wraw, wsem.at[0]),
            pltpu.make_async_copy(wd_hbm, wd_s, wsem.at[1]),
            pltpu.make_async_copy(wkv_hbm, kvraw, wsem.at[2]),
        ]
        for load in loads:
            load.start()

        def dispatch(b):
            @pl.loop(0, PER)
            def _(i):
                n = b * PER + i

                @pl.when(n == 0)
                def _():
                    pltpu.make_async_copy(out_s.at[0], a_s.at[0], drecv.at[0]).start()

                @pl.when(n > 0)
                def _():
                    pltpu.make_async_remote_copy(
                        src_ref=out_s.at[n],
                        dst_ref=a_s.at[n],
                        send_sem=dsend,
                        recv_sem=drecv.at[b],
                        device_id={"expert": chip_plus(me, n), "half": core},
                        device_id_type=MESH,
                    ).start()

        x_own = x_ref[:, pl.ds(own, HD)]

        @pl.loop(0, BATCHES)
        def _(b):
            c = lax.broadcasted_iota(jnp.int32, (ROWS, TOK), 0) + b * ROWS
            group = slot_group(c)
            spread = jnp.where(group == lax.broadcasted_iota(jnp.int32, (ROWS, TOK), 1), 1.0, 0.0)
            vals = jnp.dot(spread.astype(BF16), valt_s[...], preferred_element_type=F32)
            pick = jnp.where(vals == (c - CAP * group).astype(F32), 1.0, 0.0).astype(BF16)
            rows_out = jnp.dot(pick, x_own, preferred_element_type=F32).astype(BF16)
            out_s[pl.ds(b * PER, PER)] = rows_out.reshape(PER, CAP, HD)

            @pl.when(b < AHEAD)
            def _():
                dispatch(b)

        @pl.loop(0, CHIPS)
        def _(n):
            mask_s[n] = jnp.full((CAP, 128), mod_ref[chip_minus(me, n), 0], jnp.int32).astype(BF16)

        prow = lax.broadcasted_iota(jnp.int32, (256, 256), 0)
        pcol = lax.broadcasted_iota(jnp.int32, (256, 256), 1)
        part = jnp.where(pcol == jnp.where(prow < 128, 2 * prow, 2 * prow - 255), 1.0, 0.0).astype(BF16)
        loads[0].wait()

        @pl.loop(0, D // 128)
        def _(r):
            r0 = pl.multiple_of(r * 128, 128)
            for e in range(2):
                block = wraw[e, pl.ds(r0, 128)].reshape(256, UNITS)
                parted = jnp.dot(part, block, preferred_element_type=F32).astype(BF16)
                w_s[pl.ds(r0, 128), e * 2 * UNITS : e * 2 * UNITS + UNITS] = parted[:128]
                w_s[pl.ds(r0, 128), e * 2 * UNITS + UNITS : (e + 1) * 2 * UNITS] = parted[128:]

        loads[2].wait()

        @pl.loop(0, D // 128)
        def _(r):
            r0 = pl.multiple_of(r * 128, 128)
            block = kvraw[pl.ds(r0, 128)].reshape(256, 256)
            parted = jnp.dot(part, block, preferred_element_type=F32).astype(BF16)
            kvw_s[pl.ds(r0, 128), 0:256] = parted[:128]
            kvw_s[pl.ds(r0, 128), 256:512] = parted[128:]

        loads[1].wait()

        def forward(b):
            pltpu.make_async_copy(pieces(a_s, b), pieces(a_s, b), drecv.at[b]).wait()
            pltpu.make_async_remote_copy(
                src_ref=pieces(a_s, b),
                dst_ref=pieces(b_s, b),
                send_sem=fsend.at[b],
                recv_sem=frecv.at[b],
                device_id={"expert": me, "half": mate},
                device_id_type=MESH,
            ).start()

        def swap(b):
            return pltpu.make_async_remote_copy(
                src_ref=ps_s.at[b % 2],
                dst_ref=pr_s.at[b % 3],
                send_sem=psend.at[b % 2],
                recv_sem=precv.at[b % 3],
                device_id={"expert": me, "half": mate},
                device_id_type=MESH,
            )

        forward(0)

        @pl.loop(0, BATCHES + 1)
        def _(b):
            @pl.when(b < BATCHES - 1)
            def _():
                forward(b + 1)

            @pl.when(b < BATCHES)
            def _():
                pltpu.make_async_remote_copy(
                    src_ref=pieces(a_s, b),
                    dst_ref=pieces(b_s, b),
                    send_sem=fsend.at[b],
                    recv_sem=frecv.at[b],
                    device_id={"expert": me, "half": mate},
                    device_id_type=MESH,
                ).wait()
                xa = a_s[pl.ds(b * PER, PER)].reshape(ROWS, HD)
                xb = b_s[pl.ds(b * PER, PER)].reshape(ROWS, HD)

                @pl.loop(0, 4)
                def _(k):
                    cols = pl.ds(pl.multiple_of(k * UNITS, 128), UNITS)
                    gu_s[:, cols] = jnp.dot(
                        xa, w_s[pl.ds(own, HD), cols], preferred_element_type=F32
                    ) + jnp.dot(xb, w_s[pl.ds(oth, HD), cols], preferred_element_type=F32)

                mask = mask_s[pl.ds(b * PER, PER)].reshape(ROWS, 128).astype(F32)
                image = jnp.concatenate([mask, mask, mask], axis=1) > 0.5
                gate = jnp.where(image, gu_s[:, 2 * UNITS : 3 * UNITS], gu_s[:, :UNITS])
                up = jnp.where(image, gu_s[:, 3 * UNITS :], gu_s[:, UNITS : 2 * UNITS])
                act = gate / (1.0 + jnp.exp(-gate)) * up
                both = jnp.concatenate(
                    [jnp.where(image, 0.0, act), jnp.where(image, act, 0.0)], axis=1
                ).astype(BF16)
                ps_s[b % 2] = jnp.dot(both, wd_s[:, pl.ds(oth, HD)], preferred_element_type=F32)
                swap(b).start()
                own_s[b % 2] = jnp.dot(both, wd_s[:, pl.ds(own, HD)], preferred_element_type=F32)

            @pl.when(b > 0)
            def _():
                done = b - 1
                swap(done).wait()
                ret_s[pl.ds(done * PER, PER)] = (
                    (own_s[done % 2] + pr_s[done % 3]).astype(BF16).reshape(PER, CAP, HD)
                )

                @pl.loop(0, PER)
                def _(i):
                    n = done * PER + i

                    @pl.when(n == 0)
                    def _():
                        pltpu.make_async_copy(ret_s.at[0], rin_s.at[0], rrecv.at[0]).start()

                    @pl.when(n > 0)
                    def _():
                        pltpu.make_async_remote_copy(
                            src_ref=ret_s.at[n],
                            dst_ref=rin_s.at[n],
                            send_sem=rsend,
                            recv_sem=rrecv.at[done],
                            device_id={"expert": chip_minus(me, n), "half": core},
                            device_id_type=MESH,
                        ).start()

            @pl.when(b + AHEAD < BATCHES)
            def _():
                dispatch(b + AHEAD)

    pl.run_scoped(
        experts,
        pltpu.VMEM((2, D, 2, UNITS), BF16),
        pltpu.VMEM((D, 4 * UNITS), BF16),
        pltpu.VMEM((2 * UNITS, D), BF16),
        pltpu.VMEM((D, 2, 256), BF16),
        pltpu.VMEM((ROWS, 4 * UNITS), F32),
        pltpu.VMEM((2, ROWS, HD), F32),
        pltpu.VMEM((CHIPS, CAP, 128), BF16),
    )

    def along(i, axis):
        return 1 - ((i + 6 - axis - core) % 3 + 1) // 2

    def coordinate(axis):
        return sum(place[i] * along(i, axis) for i in range(3))

    def neighbour(axis, step):
        moved = [(place[i] + step * along(i, axis)) % 4 for i in range(3)]
        return {"expert": moved[0] * 16 + moved[1] * 4 + moved[2], "half": core}

    def send(p, view, phase, step, mark):
        pltpu.make_async_remote_copy(
            src_ref=view,
            dst_ref=view,
            send_sem=ssem.at[p, phase],
            recv_sem=rsem.at[p, mark],
            device_id=neighbour(PARTS[p][0][phase], step),
            device_id_type=MESH,
        ).start()

    def landed(p, view, mark):
        pltpu.make_async_copy(view, view, rsem.at[p, mark]).wait()

    early, late, every = pl.ds(0, 2), pl.ds(2, 2), pl.ds(0, 4)

    def one(p, shift, kinds):
        a, b, c = spots[p]
        return bufs[p].at[c, kinds, b, (a + shift) % 4]

    def line(p, shift, kinds):
        a, b, c = spots[p]
        return bufs[p].at[c, kinds, (b + shift) % 4]

    def sheet(p, shift, k, kinds):
        a, b, c = spots[p]
        return bufs[p].at[(c + shift) % 4, kinds, (b + group_shift(k)) % 4]

    def ring(view, phase, base):
        for p in range(3):
            send(p, view(p, 0, every), phase, 1, base)
            send(p, view(p, 0, every), phase, 3, base + 1)

    def pass_on(view, phase, base):
        for p in range(3):
            landed(p, view(p, 3, every), base)
            landed(p, view(p, 1, every), base + 1)
            send(p, view(p, 3, early), phase, 1, base + 2)
            send(p, view(p, 1, late), phase, 3, base + 3)

    def opposite(view, base):
        for p in range(3):
            landed(p, view(p, 2, early), base + 2)
            landed(p, view(p, 2, late), base + 3)

    def group(k):
        return lambda p, shift, kinds: sheet(p, shift, k, kinds)

    spots = [tuple(coordinate(axis) for axis in axes) for axes, _, _ in PARTS]

    def head_norm(values, gain):
        scale = lax.rsqrt(jnp.mean(values * values, axis=-1, keepdims=True) + EPSILON)
        return (values * scale * gain).astype(BF16)

    def project(wq_s, acc_s, nrm_s):
        load = pltpu.make_async_copy(wq_hbm, wq_s, wsem.at[0])
        load.start()
        acc_s[...] = x_ref[:, pl.ds(own, HD)].astype(F32)
        wide = 2 * ROWS

        @pl.loop(0, BATCHES // 2)
        def _(b):
            c = lax.broadcasted_iota(jnp.int32, (TOK, wide), 1) + b * wide
            group = slot_group(c)
            spread = jnp.where(group == lax.broadcasted_iota(jnp.int32, (TOK, wide), 0), 1.0, 0.0).astype(BF16)
            vals = jnp.dot(val_s[...], spread, preferred_element_type=F32)
            pick = vals == (c - CAP * group).astype(F32)
            w_hi = jnp.where(pick, jnp.dot(hi_s[...], spread, preferred_element_type=F32), 0.0).astype(BF16)
            w_lo = jnp.where(pick, jnp.dot(lo_s[...], spread, preferred_element_type=F32), 0.0).astype(BF16)
            for k in range(2):
                pltpu.make_async_copy(pieces(rin_s, 2 * b + k), pieces(rin_s, 2 * b + k), rrecv.at[2 * b + k]).wait()
            back = rin_s[pl.ds(b * 2 * PER, 2 * PER)].reshape(wide, HD)
            acc_s[...] += jnp.dot(w_hi, back, preferred_element_type=F32) + jnp.dot(
                w_lo, back, preferred_element_type=F32
            )

        ho_ref[:, pl.ds(own, HD)] = acc_s[...]
        share = pltpu.make_async_remote_copy(
            src_ref=acc_s,
            dst_ref=ho_ref.at[:, pl.ds(own, HD)],
            send_sem=hsend,
            recv_sem=hrecv,
            device_id={"expert": me, "half": mate},
            device_id_type=MESH,
        )
        share.start()
        share.wait()
        hidden = ho_ref[...]
        mean_sq = jnp.mean(hidden * hidden, axis=-1, keepdims=True)
        nrm_s[...] = (hidden * lax.rsqrt(mean_sq + EPSILON) * gain_ref[...]).astype(BF16)


        for group_of in range(2):
            pair = jnp.dot(
                nrm_s[...], kvw_s[:, group_of * 256 : (group_of + 1) * 256], preferred_element_type=F32
            )
            for i in range(2):
                rows_kv = pair[:, i * 128 : (i + 1) * 128]
                rows_kv = head_norm(rows_kv, kg_ref[...]) if group_of == 0 else rows_kv.astype(BF16)
                for p, (_, rows, first) in enumerate(PARTS):
                    a, b, c = spots[p]
                    bufs[p][c, 2 * group_of + i, b, a] = rows_kv[first : first + rows]
        ring(one, 0, 0)
        load.wait()

        def queries(first, last):
            @pl.loop(first, last)
            def _(k):
                cols = pl.ds(pl.multiple_of(k * 256, 256), 256)
                q2 = jnp.dot(nrm_s[...], wq_s[:, cols], preferred_element_type=F32)
                for i in range(2):
                    rows_q = pl.ds(pl.multiple_of((2 * (k % 4) + i) * 128, 128), 128)
                    q_s[k // 4, rows_q] = head_norm(q2[:, i * 128 : (i + 1) * 128], qg_ref[...])

        queries(0, 3)
        pass_on(one, 0, 0)
        queries(3, 5)
        opposite(one, 0)
        ring(line, 1, 4)
        ring(group(0), 2, 8)
        queries(5, 8)

    pl.run_scoped(
        project, pltpu.VMEM((D, D), BF16), pltpu.VMEM((TOK, HD), F32), pltpu.VMEM((TOK, D), BF16)
    )

    pass_on(line, 1, 4)
    ring(group(1), 2, 12)
    ring(group(2), 2, 16)

    def attend(kun, vun, vt_s, s0, s1, m_s, sum_s):
        m_s[...] = jnp.full_like(m_s, -1e30)
        sum_s[...] = jnp.zeros_like(sum_s)
        vt_s[:, 128:, :] = jnp.ones((2, VROWS - 128, KEYS), BF16)
        scale = 128**-0.5 * LOG2E

        def scores(h, r):
            cols = pl.ds(pl.multiple_of(r * QCOLS, QCOLS), QCOLS)
            return lax.dot_general(kun[h], q_s[h, cols], (((1,), (1,)), ((), ())), preferred_element_type=F32)

        def absorb(h, s_ref, r):
            cols = pl.ds(pl.multiple_of(r * QCOLS, QCOLS), QCOLS)
            s = s_ref[...]
            m_old = m_s[h, :, cols]
            m_new = jnp.maximum(m_old, jnp.max(s, axis=0, keepdims=True))
            m_s[h, :, cols] = m_new
            probs = jnp.exp2(s * scale - m_new * scale).astype(BF16)
            fade = jnp.exp2((m_old - m_new) * scale)
            sum_s[h, :, cols] = sum_s[h, :, cols] * fade + jnp.dot(vt_s[h], probs, preferred_element_type=F32)

        steps = q_s.shape[1] // QCOLS

        @pl.loop(0, UNITS_KV)
        def _(u):
            @pl.when(u == 1)
            def _():
                opposite(line, 4)
                ring(group(3), 2, 20)

            for k in range(4):

                @pl.when(u == 2 + k)
                def _(k=k):
                    pass_on(group(k), 2, 8 + 4 * k)

            for k in range(2):

                @pl.when(u == 6 + k)
                def _(k=k):
                    opposite(group(2 * k), 8 + 8 * k)
                    opposite(group(2 * k + 1), 12 + 8 * k)

            stage = u // 2
            mid = (stage % 3 + 1) // 2
            start = 0
            for p, (axes, rows, first) in enumerate(PARTS):
                a, b, c = spots[p]
                for i in range(2):
                    shift_c = (1 - mid) * 2 * (stage // 3) + mid * (3 - 2 * i)
                    k = (1 - mid) * (2 * (u % 2) + i) + mid * (u - 2)
                    at_c, at_b = (c + shift_c) % 4, (b + group_shift(k)) % 4
                    for h in range(2):
                        kun[h, start : start + 4 * rows] = bufs[p][at_c, h, at_b].reshape(4 * rows, 128)
                        vun[h, start : start + 4 * rows] = bufs[p][at_c, 2 + h, at_b].reshape(4 * rows, 128)
                    start += 4 * rows
            for h in range(2):
                vt_s[h, :128, :] = vun[h].T

            s0[...] = scores(0, 0)

            @pl.loop(0, steps)
            def _(r):
                s1[...] = scores(1, r)
                absorb(0, s0, r)
                s0[...] = scores(0, lax.rem(r + 1, steps))
                absorb(1, s1, r)

        for h in range(2):
            for j in range(8):
                cols = slice(j * 128, (j + 1) * 128)
                head = sum_s[h, :128, cols] / sum_s[h, 128:129, cols]
                att_ref[:, (h * 8 + j) * 128 : (h * 8 + j + 1) * 128] = head.T.astype(BF16)


    pl.run_scoped(
        attend,
        pltpu.VMEM((2, KEYS, 128), BF16),
        pltpu.VMEM((2, KEYS, 128), BF16),
        pltpu.VMEM((2, VROWS, KEYS), BF16),
        pltpu.VMEM((KEYS, QCOLS), F32),
        pltpu.VMEM((KEYS, QCOLS), F32),
        pltpu.VMEM((2, 1, 1024), F32),
        pltpu.VMEM((2, VROWS, 1024), F32),
    )

    three = pl.ds(0, 3)
    for p in range(3):
        a, b, c = spots[p]
        view = bufs[p].at[c, :, b, three]
        pltpu.make_async_copy(view, view, ssem.at[p, 0]).wait()
        view = bufs[p].at[c, :, three]
        pltpu.make_async_copy(view, view, ssem.at[p, 1]).wait()
        view = bufs[p].at[three]
        pltpu.make_async_copy(view, view, ssem.at[p, 2]).wait()
    rest = pl.ds(1, CHIPS - 1)
    pltpu.make_async_copy(out_s.at[rest], out_s.at[rest], dsend).wait()
    pltpu.make_async_copy(ret_s.at[rest], ret_s.at[rest], rsend).wait()


def layer_call(x, mod, ids, rw, wgu, wd, gain, wq, wkv, qg, kg):
    vm = pl.BlockSpec(memory_space=pltpu.VMEM)
    hbm = pl.BlockSpec(memory_space=pl.ANY)
    sm = pl.BlockSpec(memory_space=pltpu.SMEM)
    dma = pltpu.SemaphoreType.DMA
    return pl.pallas_call(
        layer_kernel,
        out_shape=(jax.ShapeDtypeStruct((TOK, D), F32), jax.ShapeDtypeStruct((TOK, D), BF16)),
        in_specs=[vm, sm, vm, vm, hbm, hbm, vm, hbm, hbm, vm, vm],
        out_specs=(vm, vm),
        scratch_shapes=[
            pltpu.VMEM((D, 512), BF16),
            pltpu.VMEM((CHIPS, CAP, HD), BF16),
            pltpu.VMEM((CHIPS, CAP, HD), BF16),
            pltpu.VMEM((CHIPS, CAP, HD), BF16),
            pltpu.VMEM((CHIPS, CAP, HD), BF16),
            pltpu.VMEM((CHIPS, CAP, HD), BF16),
            pltpu.VMEM((2, ROWS, HD), F32),
            pltpu.VMEM((3, ROWS, HD), F32),
            pltpu.VMEM((TOK, TOK), BF16),
            pltpu.VMEM((TOK, TOK), BF16),
            pltpu.VMEM((TOK, TOK), BF16),
            pltpu.VMEM((TOK, TOK), BF16),
            pltpu.VMEM((2, 8 * TOK, 128), BF16),
        ]
        + [pltpu.VMEM((4, 4, 4, 4, rows, 128), BF16) for _, rows, _ in PARTS]
        + [
            dma((3,)),
            dma,
            dma((BATCHES,)),
            dma((BATCHES,)),
            dma((BATCHES,)),
            dma((2,)),
            dma((3,)),
            dma,
            dma((BATCHES,)),
            dma,
            dma,
            dma((3, 3)),
            dma((3, 24)),
        ],
        compiler_params=pltpu.CompilerParams(
            collective_id=0, has_side_effects=True, vmem_limit_bytes=54260000
        ),
    )(x, mod, ids, rw, wgu, wd, gain, wq, wkv, qg, kg)


def body(hidden_in, modality, expert_ids, route_weights, w_gate_up, w_down, norm_gain, w_query,
         key_value_weight, q_gain, k_gain):
    return layer_call(
        hidden_in, modality.reshape(CHIPS, TOK), expert_ids.T, route_weights.T, w_gate_up,
        w_down.reshape(2 * UNITS, D), norm_gain.reshape(1, D), w_query, key_value_weight,
        q_gain.reshape(1, 128), k_gain.reshape(1, 128),
    )


def solution(mesh):
    in_specs = (
        P("expert", None), P(), P("expert", None), P("expert", None),
        P("expert", None, None, "half"), P("expert", "half", None), P(), P(None, "half"),
        P(None, None, "half"), P(), P(),
    )
    out_specs = (P("expert", None), P("expert", "half"))
    return jax.shard_map(body, mesh=mesh, in_specs=in_specs, out_specs=out_specs, check_vma=False)
```
